256 devices in a mesh: plane: 4 (over z_hi), mode: 64 (over x, y, z_lo, core).
Axes of the slice: x: 4, y: 4, z: 8 (z_hi: 4, z_lo: 2; z = z_hi * 2 + z_lo), core: 2. Of those that a mesh axis runs over, the one named last changes fastest.
Arguments:
- phase_masks: float32 [4, 512, 512], P('plane'), may hold values from -3.140625 to 3.140625
- hg_orders: int32 [256, 2], P('mode'), may hold values from 0 to 44
- spot_index: int32 [256], P('mode'), may hold values from 0 to 1023
Outputs:
- phase_next: float32 [4, 512, 512], P('plane')
The draws below stay inside these ranges and needn't reach their ends.
Inputs may be any that keep to these rules, and one draw needn't show every extreme that they name: `spot_index`: the output spot of each mode; several modes may share a spot.
All inputs are finite; a program needn't handle non-finite values.
Results may differ from the reference program's by a relative error of at most 0.018.
Values may be sent and summed in bfloat16 or wider, within the bound.
No kernel may reach another device: no remote copies, remote signals or barrier semaphores. Data moves between devices by JAX's collectives and lax.ppermute only.
A program may use at most 64 MiB of HBM per device.

```python
import math
import jax
import jax.numpy as jnp
from jax import lax

N = 512
ORDERS = 45
SPOT_SIDE = 32
PLANES = 4
MODES = 256
SPOTS = 1024


def place_ends(drawn, stream_key, low, top_value):
    dims = drawn.shape
    spot = [jax.random.randint(jax.random.fold_in(stream_key, axis), (), 0, dims[axis]) for axis in range(len(dims))]
    drawn = drawn.at[tuple(spot)].set(low)
    longest = dims.index(max(dims))
    spot[longest] = (spot[longest] + 1) % dims[longest]
    return drawn.at[tuple(spot)].set(top_value)


def setup_inputs(seed: int = 0) -> dict:
    streams_of = jax.random.split(jax.random.key(seed), 4)
    phase_masks = jnp.clip(jax.random.uniform(streams_of[0], (PLANES, N, N), jnp.float32, -3.140625, 3.140625), -3.140625, 3.140625)
    hg_orders = place_ends(jax.random.randint(streams_of[1], (MODES, 2), 0, ORDERS), jax.random.fold_in(streams_of[1], 1), 0, ORDERS - 1).astype(jnp.int32)
    spot_index = place_ends(jax.random.randint(streams_of[2], (MODES,), 0, SPOTS), jax.random.fold_in(streams_of[2], 1), 0, SPOTS - 1).astype(jnp.int32)
    return {"phase_masks": phase_masks, "hg_orders": hg_orders, "spot_index": spot_index}


CHIRP_RATE = math.pi / 48.0 * (math.pi / 48.0)
AMPLITUDE = 12.0
EPSILON = 1e-06

def kernel_parts(extent):
    positions = jnp.arange(extent, dtype=jnp.int32)
    centred = (positions + extent // 2) % extent - extent // 2
    wrapped = positions[:, None] * positions[None, :] % extent
    chirp_phase = CHIRP_RATE * (centred * centred).astype(jnp.float32)
    angles = 2.0 * math.pi / extent * wrapped.astype(jnp.float32) - chirp_phase[None, :]
    kernel_re = lax.optimization_barrier(jnp.sum(jnp.cos(angles), axis=1)) / extent
    kernel_im = lax.optimization_barrier(jnp.sum(jnp.sin(angles), axis=1)) / extent
    return (kernel_re, kernel_im)

def circulant(values):
    extent = values.shape[0]
    repeated = jnp.tile(values, extent + 1)
    hankel = repeated.reshape(extent, extent + 1)[:, :extent]
    return jnp.roll(jnp.flip(hankel, 1), 1, 1)

def operators(extent):
    kernel_re, kernel_im = kernel_parts(extent)
    matrix_re = circulant(kernel_re)
    matrix_im = circulant(kernel_im)
    prop_re = matrix_re.astype(jnp.bfloat16)
    prop_im = matrix_im.astype(jnp.bfloat16)
    forward_mats = (prop_re, prop_im, (matrix_re + matrix_im).astype(jnp.bfloat16))
    backward_mats = (prop_re, -prop_im, (matrix_re - matrix_im).astype(jnp.bfloat16))
    return (forward_mats, backward_mats)

def left_product(left_re, left_im, left_sum, field_re, field_im):
    field_sum = (field_re.astype(jnp.float32) + field_im.astype(jnp.float32)).astype(jnp.bfloat16)
    first_term = jnp.dot(left_re, field_re, preferred_element_type=jnp.float32)
    second_term = jnp.dot(left_im, field_im, preferred_element_type=jnp.float32)
    third_term = jnp.dot(left_sum, field_sum, preferred_element_type=jnp.float32)
    return (first_term - second_term, third_term - first_term - second_term)

def right_product(field_re, field_im, right_re, right_im, right_sum):
    field_sum = (field_re.astype(jnp.float32) + field_im.astype(jnp.float32)).astype(jnp.bfloat16)
    first_term = jnp.dot(field_re, right_re, preferred_element_type=jnp.float32)
    second_term = jnp.dot(field_im, right_im, preferred_element_type=jnp.float32)
    third_term = jnp.dot(field_sum, right_sum, preferred_element_type=jnp.float32)
    return (first_term - second_term, third_term - first_term - second_term)

def propagate(field_re, field_im, matrices):
    matrix_re, matrix_im, matrix_sum = matrices
    middle_re, middle_im = left_product(matrix_re, matrix_im, matrix_sum, field_re, field_im)
    middle_re, middle_im = lax.optimization_barrier((middle_re.astype(jnp.bfloat16), middle_im.astype(jnp.bfloat16)))
    return right_product(middle_re, middle_im, matrix_re, matrix_im, matrix_sum)

def hermite(orders, extent):
    scaled = (jnp.arange(extent, dtype=jnp.float32) - (extent - 1) / 2.0) / (extent / 48.0)
    lowest = math.pow(math.pi, -0.25) * jnp.exp(-0.5 * scaled * scaled)
    second = math.sqrt(2.0) * scaled * lowest
    chosen = jnp.where((orders == 0)[:, None], lowest[None, :], 0.0)
    chosen = jnp.where((orders == 1)[:, None], second[None, :], chosen)

    def advance(degree, carried):
        previous, current, picked = carried
        degree_f = degree.astype(jnp.float32)
        higher = jnp.sqrt(2.0 / (degree_f + 1.0)) * scaled * current - jnp.sqrt(degree_f / (degree_f + 1.0)) * previous
        picked = jnp.where((orders == degree + 1)[:, None], higher[None, :], picked)
        return (current, higher, picked)
    previous, current, chosen = lax.fori_loop(1, ORDERS - 1, advance, (lowest, second, chosen))
    return chosen

def spot_profile(spots, extent):
    coords = jnp.arange(extent, dtype=jnp.float32) - (extent - 1) / 2.0
    spacing = extent / 40.0
    spot_width = extent / 120.0
    centre = (SPOT_SIDE - 1) / 2.0
    spot_row = (spots // SPOT_SIDE).astype(jnp.float32) - centre
    spot_col = (spots % SPOT_SIDE).astype(jnp.float32) - centre
    offset_x = (coords[None, :] - spacing * spot_row[:, None]) / spot_width
    offset_y = (coords[None, :] - spacing * spot_col[:, None]) / spot_width
    return (jnp.exp(-offset_x * offset_x), jnp.exp(-offset_y * offset_y))

def mode_tables(orders, spots, extent):
    profile_x, profile_y = spot_profile(spots, extent)
    return (AMPLITUDE * hermite(orders[:, 0], extent), hermite(orders[:, 1], extent), profile_x, profile_y)

def apply_mask(field_re, field_im, cos_mask, sin_mask):
    masked_re = (field_re * cos_mask - field_im * sin_mask).astype(jnp.bfloat16)
    masked_im = (field_re * sin_mask + field_im * cos_mask).astype(jnp.bfloat16)
    return lax.optimization_barrier((masked_re, masked_im))

def remove_mask(back_re, back_im, cos_mask, sin_mask):
    reply_re = (back_re * cos_mask + back_im * sin_mask).astype(jnp.bfloat16)
    reply_im = (back_im * cos_mask - back_re * sin_mask).astype(jnp.bfloat16)
    return lax.optimization_barrier((reply_re, reply_im))

def whole_mode(input_x, input_y, target, cos_masks, sin_masks, forward_mats, backward_mats):
    plane_count = cos_masks.shape[0]
    field_re = input_x[:, None] * input_y[None, :]
    field_im = jnp.zeros_like(field_re)
    masked_fields = []
    for plane_at in range(plane_count):
        masked_re, masked_im = apply_mask(field_re, field_im, cos_masks[plane_at], sin_masks[plane_at])
        masked_fields.append((masked_re, masked_im))
        out_re, out_im = propagate(masked_re, masked_im, forward_mats)
        rounded = lax.optimization_barrier((out_re.astype(jnp.bfloat16), out_im.astype(jnp.bfloat16)))
        field_re = rounded[0].astype(jnp.float32)
        field_im = rounded[1].astype(jnp.float32)
    coupling_re = jnp.sum(target * out_re)
    coupling_im = jnp.sum(target * out_im)
    source_re, source_im = lax.optimization_barrier(((coupling_re * target).astype(jnp.bfloat16), (coupling_im * target).astype(jnp.bfloat16)))
    grad_terms = []
    for plane_at in reversed(range(plane_count)):
        back_re, back_im = propagate(source_re, source_im, backward_mats)
        masked_re, masked_im = masked_fields[plane_at]
        grad_terms.append(2.0 * (back_im * masked_re.astype(jnp.float32) - back_re * masked_im.astype(jnp.float32)))
        source_re, source_im = remove_mask(back_re, back_im, cos_masks[plane_at], sin_masks[plane_at])
    return jnp.stack(grad_terms[::-1])

def reference(phase_masks, hg_orders, spot_index):
    extent = phase_masks.shape[1]
    plane_count = phase_masks.shape[0]
    forward_mats, backward_mats = operators(extent)
    cos_masks = jnp.cos(phase_masks)
    sin_masks = jnp.sin(phase_masks)
    tables = mode_tables(hg_orders, spot_index, extent)

    def one_mode(grad_total, entries):
        input_x, input_y, profile_x, profile_y = entries
        target = profile_x[:, None] * profile_y[None, :]
        return (grad_total + whole_mode(input_x, input_y, target, cos_masks, sin_masks, forward_mats, backward_mats), None)
    grad_total, unused = lax.scan(one_mode, jnp.zeros((plane_count, extent, extent), jnp.float32), tables)
    mean_square = lax.optimization_barrier(jnp.mean(grad_total * grad_total, axis=(1, 2), keepdims=True))
    return phase_masks + grad_total / jnp.sqrt(mean_square + EPSILON)
```

```python
import functools
import math

import jax
import jax.numpy as jnp
import numpy as np
from jax import lax
from jax.experimental import pallas as pl
from jax.experimental.pallas import tpu as pltpu
from jax.sharding import Mesh
from jax.sharding import PartitionSpec as P

ORDERS = 45
SPOT_SIDE = 32
MODE = ("mode_0", "mode_1", "mode_2", "mode_3")
XY = ("mode_0", "mode_1")
Z = ("plane", "mode_2")
CORE = "mode_3"
XY_DEVICES = 16
PLANES = 4
N = 512
B = 128
STRIP = 16
CHIRP_RATE = math.pi / 48.0 * (math.pi / 48.0)
AMPLITUDE = 12.0
EPSILON = 1e-06
F32 = jnp.float32
BF16 = jnp.bfloat16


def block_operators():
    f = np.arange(N)
    s = (f + N // 2) % N - N // 2
    chirp = np.exp(-1j * CHIRP_RATE * s.astype(np.float64) ** 2)
    phase = np.exp(2j * np.pi * ((f[:, None] * f[None, :]) % N) / N)
    kernel = (phase * chirp[None, :]).sum(axis=1) / N
    offset = np.arange(B)[:, None] - np.arange(B)[None, :]
    left, right = [], []
    for k in range(4):
        block = sum((-1j) ** (k * m) * kernel[(offset + B * m) % N] for m in range(4)) / 4.0
        real = np.block([[block.real, -block.imag], [block.imag, block.real]])
        left.append(real)
        right.append(real.T)
    to = lambda x: jnp.asarray(np.stack(x).astype(np.float32)).astype(BF16)
    return to(left), to(right)


def add(x, y):
    return (x[0] + y[0], x[1] + y[1])


def sub(x, y):
    return (x[0] - y[0], x[1] - y[1])


def turned(x, y):
    return (x[0] - y[1], x[1] + y[0])


def turned_back(x, y):
    return (x[0] + y[1], x[1] - y[0])


def dft4(x):
    a, b, c, d = add(x[0], x[2]), sub(x[0], x[2]), add(x[1], x[3]), sub(x[1], x[3])
    return [add(a, c), turned_back(b, d), sub(a, c), turned(b, d)]


def idft4(x):
    a, b, c, d = add(x[0], x[2]), sub(x[0], x[2]), add(x[1], x[3]), sub(x[1], x[3])
    return [add(a, c), turned(b, d), sub(a, c), turned_back(b, d)]


def both_ways(grid, transform):
    grid = [transform(row) for row in grid]
    cols = [transform([grid[k][l] for k in range(4)]) for l in range(4)]
    return [[cols[l][k] for l in range(4)] for k in range(4)]


def mul(x, y):
    return (x[0] * y[0] - x[1] * y[1], x[0] * y[1] + x[1] * y[0])


def dot(a, b):
    return jnp.dot(a, b, preferred_element_type=F32)


def lanes(l):
    return slice(l * B, (l + 1) * B)


def hermite_tables(psi):
    t = (lax.broadcasted_iota(jnp.int32, (8, N), 1).astype(F32) - (N - 1) / 2.0) / (N / 48.0)
    previous = math.pow(math.pi, -0.25) * jnp.exp(-0.5 * t * t)
    current = math.sqrt(2.0) * t * previous
    psi[0] = previous
    psi[1] = current
    for n in range(1, ORDERS - 1):
        higher = math.sqrt(2.0 / (n + 1.0)) * t * current - math.sqrt(n / (n + 1.0)) * previous
        psi[n + 1] = higher
        previous, current = current, higher


def spot_profile(index, shape, dim):
    coords = lax.broadcasted_iota(jnp.int32, shape, dim).astype(F32) - (N - 1) / 2.0
    centre = index.astype(F32) - (SPOT_SIDE - 1) / 2.0
    offset = (coords - (N / 40.0) * centre) / (N / 120.0)
    return jnp.exp(-offset * offset)


def split(x):
    high = x.astype(BF16)
    return high, (x - high.astype(F32)).astype(BF16)


def main_kernel(
    orders, spots, pick, half_own, half_other, left, right, keep, send,
    psi, source_x, far_x, x_ref, v_ref, y_ref, g_ref, mask_ref, tan_ref, grad, sems,
):
    mode, core = pick[0], pick[1]
    arrivals = [
        pltpu.make_async_copy(half_own, tan_ref.at[core], sems.at[0]),
        pltpu.make_async_copy(half_other, tan_ref.at[1 - core], sems.at[1]),
    ]
    for copy in arrivals:
        copy.start()
    hermite_tables(psi)
    source_y = psi[orders[mode, 1]]
    row = AMPLITUDE * psi[orders[mode, 0]][0:1]
    for k in range(4):
        source_x[k * B : (k + 1) * B, :] = jnp.broadcast_to(row[:, lanes(k)], (B, B)).T

    spot = spots[mode]
    down = spot_profile(spot // SPOT_SIDE, (N, B), 0)
    zero = jnp.zeros((B, B), F32)
    spread = dft4([(down[k * B : (k + 1) * B], zero) for k in range(4)])
    moved = []
    for k in range(4):
        high, low = split(jnp.concatenate(spread[k], axis=0))
        both = dot(left[k], jnp.concatenate([high, low], axis=1))
        total = both[:, :B] + both[:, B:]
        moved.append((total[:B], total[B:]))
    for k, part in enumerate(idft4(moved)):
        far_x[0, k * B : (k + 1) * B, :] = part[0]
        far_x[1, k * B : (k + 1) * B, :] = part[1]
    along = spot_profile(spot % SPOT_SIDE, (8, N), 1)
    zero = jnp.zeros((8, B), F32)
    spread = dft4([(along[:, lanes(l)], zero) for l in range(4)])
    moved = []
    for l in range(4):
        high, low = split(jnp.concatenate(spread[l], axis=1))
        both = dot(jnp.concatenate([high, low], axis=0), right[l])
        total = both[:8] + both[8:]
        moved.append((total[:, :B], total[:, B:]))
    far_y = idft4(moved)

    def rows_of(k, s):
        return pl.ds(k * B + s * STRIP, STRIP)

    def mask_at(plane, k, l, s):
        t = tan_ref[k // 2, (k % 2) * (B // STRIP) + s, plane, :, lanes(l)].astype(F32)
        twice = 2.0 / (1.0 + t * t)
        mask = (twice - 1.0, twice * t)
        if plane:
            mask_ref[plane - 1, 0, rows_of(k, s), lanes(l)] = mask[0]
            mask_ref[plane - 1, 1, rows_of(k, s), lanes(l)] = mask[1]
        return mask

    def kept_mask_at(plane, k, l, s):
        at = mask_ref.at[plane - 1]
        return (at[0, rows_of(k, s), lanes(l)], at[1, rows_of(k, s), lanes(l)])

    def spread_out(grid, s):
        grid = both_ways(grid, dft4)
        for k in range(4):
            for l in range(4):
                x_ref[k, pl.ds(s * STRIP, STRIP), lanes(l)] = grid[k][l][0].astype(BF16)
                x_ref[k, pl.ds(B + s * STRIP, STRIP), lanes(l)] = grid[k][l][1].astype(BF16)

    def gathered_up(s):
        grid = [
            [(y_ref[l, rows_of(k, s), 0:B], y_ref[l, rows_of(k, s), B : 2 * B]) for l in range(4)]
            for k in range(4)
        ]
        return both_ways(grid, idft4)

    def operate():
        for k in range(4):
            z = dot(left[k], x_ref[k]).astype(BF16)
            for l in range(4):
                v_ref[l, k * B : (k + 1) * B, 0:B] = z[:B, lanes(l)]
                v_ref[l, k * B : (k + 1) * B, B : 2 * B] = z[B:, lanes(l)]
        for l in range(4):
            y_ref[l] = dot(v_ref[l], right[l])

    def masked(plane, field, k, l, s):
        g = mul(field, mask_at(plane, k, l, s))
        g_ref[plane, 0, rows_of(k, s), lanes(l)] = g[0].astype(BF16)
        g_ref[plane, 1, rows_of(k, s), lanes(l)] = g[1].astype(BF16)
        return g

    def first_strip(s, carry):
        def at(k, l):
            field = source_x[rows_of(k, s), :] * source_y[0:1, lanes(l)]
            mask = mask_at(0, k, l, s)
            g = (field * mask[0], field * mask[1])
            g_ref[0, 0, rows_of(k, s), lanes(l)] = g[0].astype(BF16)
            g_ref[0, 1, rows_of(k, s), lanes(l)] = g[1].astype(BF16)
            return g

        spread_out([[at(k, l) for l in range(4)] for k in range(4)], s)
        return carry

    def forward_strip(plane, s, carry):
        field = gathered_up(s)
        spread_out([[masked(plane, field[k][l], k, l, s) for l in range(4)] for k in range(4)], s)
        return carry

    def last_strip(s, carry):
        field = gathered_up(s)
        carry = list(carry)
        for k in range(4):
            a = (far_x[0, rows_of(k, s), :], far_x[1, rows_of(k, s), :])
            for l in range(4):
                carry[l] = add(carry[l], mul(masked(PLANES - 1, field[k][l], k, l, s), a))
        return tuple(carry)

    def returned(plane, back, k, l, s):
        g = (
            g_ref[plane, 0, rows_of(k, s), lanes(l)].astype(F32),
            g_ref[plane, 1, rows_of(k, s), lanes(l)].astype(F32),
        )
        term = -2.0 * (back[0] * g[1] + back[1] * g[0])
        grad[k // 2, (k % 2) * (B // STRIP) + s, plane, :, lanes(l)] = term.astype(BF16)
        return mul(back, kept_mask_at(plane, k, l, s)) if plane else None

    strips = B // STRIP
    for copy in arrivals:
        copy.wait()
    lax.fori_loop(0, strips, first_strip, 0)
    for plane in range(1, PLANES - 1):
        operate()
        lax.fori_loop(0, strips, functools.partial(forward_strip, plane), 0)
    operate()
    nothing = jnp.zeros((STRIP, B), F32)
    sums = lax.fori_loop(0, strips, last_strip, tuple((nothing, nothing) for _ in range(4)))
    total = [mul((s[0][:8] + s[0][8:], s[1][:8] + s[1][8:]), y) for s, y in zip(sums, far_y)]
    coupling_re = jnp.sum(sum(t[0] for t in total))
    coupling_im = jnp.sum(sum(t[1] for t in total))
    back_y = [
        (coupling_re * y[0] + coupling_im * y[1], coupling_re * y[1] - coupling_im * y[0]) for y in far_y
    ]

    def turn_strip(s, carry):
        def at(k, l):
            a = (far_x[0, rows_of(k, s), :], far_x[1, rows_of(k, s), :])
            back = mul(a, (back_y[l][0][0:1], back_y[l][1][0:1]))
            return returned(PLANES - 1, back, k, l, s)

        spread_out([[at(k, l) for l in range(4)] for k in range(4)], s)
        return carry

    def backward_strip(plane, s, carry):
        back = gathered_up(s)
        reply = [[returned(plane, back[k][l], k, l, s) for l in range(4)] for k in range(4)]
        if plane:
            spread_out(reply, s)
        return carry

    lax.fori_loop(0, strips, turn_strip, 0)
    for plane in reversed(range(PLANES - 1)):
        operate()
        lax.fori_loop(0, strips, functools.partial(backward_strip, plane), 0)
    departures = [
        pltpu.make_async_copy(grad.at[core], keep, sems.at[0]),
        pltpu.make_async_copy(grad.at[1 - core], send, sems.at[1]),
    ]
    for copy in departures:
        copy.start()
    for copy in departures:
        copy.wait()


def main_call(orders, spots, pick, half_own, half_other, left, right):
    smem = pl.BlockSpec(memory_space=pltpu.SMEM)
    vmem = pl.BlockSpec(memory_space=pltpu.VMEM)
    hbm = pl.BlockSpec(memory_space=pl.ANY)
    half = (XY_DEVICES, PLANES, STRIP, N)
    return pl.pallas_call(
        main_kernel,
        name="modes",
        in_specs=[smem, smem, smem, hbm, hbm, vmem, vmem],
        out_specs=[hbm, hbm],
        out_shape=[jax.ShapeDtypeStruct(half, BF16)] * 2,
        scratch_shapes=[
            pltpu.VMEM((ORDERS, 8, N), F32),
            pltpu.VMEM((N, B), F32),
            pltpu.VMEM((2, N, B), F32),
            pltpu.VMEM((4, 2 * B, N), BF16),
            pltpu.VMEM((4, N, 2 * B), BF16),
            pltpu.VMEM((4, N, 2 * B), F32),
            pltpu.VMEM((PLANES, 2, N, N), BF16),
            pltpu.VMEM((PLANES - 1, 2, N, N), F32),
            pltpu.VMEM((2, *half), BF16),
            pltpu.VMEM((2, *half), BF16),
            pltpu.SemaphoreType.DMA((2,)),
        ],
    )(orders, spots, pick, half_own, half_other, left, right)


def tangent_kernel(where, phase, out):
    half_angle = 0.5 * phase[0]
    out[...] = (jnp.sin(half_angle) / jnp.cos(half_angle)).astype(BF16)


def tangent_call(where, phase_masks):
    return pl.pallas_call(
        tangent_kernel,
        name="tangent",
        grid_spec=pltpu.PrefetchScalarGridSpec(
            num_scalar_prefetch=1,
            grid=(1,),
            in_specs=[pl.BlockSpec((1, STRIP, N), lambda i, w: (0, w[0], 0))],
            out_specs=pl.BlockSpec((STRIP, N), lambda i, w: (0, 0)),
        ),
        out_shape=jax.ShapeDtypeStruct((STRIP, N), BF16),
    )(where, phase_masks)


def finish_kernel(pick, phase, own, other, out):
    squares = jnp.zeros((STRIP, N), F32)
    for g in range(XY_DEVICES):
        for part in (own, other):
            x = part[g].astype(F32)
            squares += x * x
    scale = lax.rsqrt(jnp.sum(squares, keepdims=True) / (N * N) + EPSILON)
    core = pick[1]
    for part, half in ((own, core), (other, 1 - core)):
        for g in range(XY_DEVICES):
            rows = pl.ds(half * (N // 2) + g * STRIP, STRIP)
            out[0, rows, :] = phase[0, rows, :] + part[g].astype(F32) * scale


def finish_call(pick, phase_masks, own, other):
    smem = pl.BlockSpec(memory_space=pltpu.SMEM)
    vmem = pl.BlockSpec(memory_space=pltpu.VMEM)
    return pl.pallas_call(
        finish_kernel,
        name="finish",
        in_specs=[smem, vmem, vmem, vmem],
        out_specs=vmem,
        out_shape=jax.ShapeDtypeStruct((1, N, N), F32),
    )(pick, phase_masks, own, other)


def swapped(x):
    return lax.ppermute(x, CORE, [(0, 1), (1, 0)])


def exchanged(x, axes):
    return lax.all_to_all(x, axes, split_axis=0, concat_axis=0, tiled=True)


def from_everyone(x, axes):
    count = lax.axis_size(axes)
    return exchanged(jnp.broadcast_to(x[None], (count, *x.shape)), axes)


def shards(phase_masks, hg_orders, spot_index):
    plane, core = lax.axis_index("plane"), lax.axis_index(CORE)
    group = core * XY_DEVICES + lax.axis_index(XY)
    pick = jnp.stack([plane, core]).astype(jnp.int32)
    tangent = tangent_call(group.astype(jnp.int32)[None], phase_masks)
    all_planes = from_everyone(tangent, "plane")
    half_own = from_everyone(all_planes, XY)
    half_other = swapped(half_own)
    left, right = block_operators()
    keep, send = main_call(hg_orders, spot_index, pick, half_own, half_other, left, right)
    pair = keep + swapped(send)
    column = jnp.sum(exchanged(pair, XY).astype(F32), axis=0).astype(BF16)
    pieces = jnp.repeat(column, 2, axis=0)
    total = jnp.sum(exchanged(pieces, Z).astype(F32), axis=0).astype(BF16)
    own = from_everyone(total, XY)
    other = swapped(own)
    return finish_call(pick, phase_masks, own, other)


def solution(mesh):
    finer = Mesh(
        mesh.devices.reshape(mesh.shape["plane"], 4, 4, 2, 2),
        ("plane", "mode_0", "mode_1", "mode_2", "mode_3"),
    )
    placed = (P("plane", None, None), P(MODE, None), P(MODE))
    return jax.shard_map(
        shards, mesh=finer, in_specs=placed, out_specs=P("plane", None, None), check_vma=False
    )
```

```python
import functools
import math

import jax
import jax.numpy as jnp
import numpy as np
from jax import lax
from jax.experimental import pallas as pl
from jax.experimental.pallas import tpu as pltpu
from jax.sharding import Mesh
from jax.sharding import PartitionSpec as P

ORDERS = 45
SPOT_SIDE = 32
MODE = ("mode_0", "mode_1", "mode_2", "mode_3")
XY = ("mode_0", "mode_1")
CHIPS = ("mode_0", "mode_1", "mode_2")
CORE = "mode_3"
XY_DEVICES = 16
PLANES = 4
N = 512
B = 128
STRIP = 16
HALF_STRIPS = N // STRIP // 2
CHIRP_RATE = math.pi / 48.0 * (math.pi / 48.0)
AMPLITUDE = 12.0
EPSILON = 1e-06
F32 = jnp.float32
BF16 = jnp.bfloat16
SMEM = pl.BlockSpec(memory_space=pltpu.SMEM)
VMEM = pl.BlockSpec(memory_space=pltpu.VMEM)
ANY = pl.BlockSpec(memory_space=pl.ANY)


def vmem_limit(mib):
    return pltpu.CompilerParams(vmem_limit_bytes=mib << 20)


def block_operators():
    f = np.arange(N)
    s = (f + N // 2) % N - N // 2
    chirp = np.exp(-1j * CHIRP_RATE * s.astype(np.float64) ** 2)
    phase = np.exp(2j * np.pi * ((f[:, None] * f[None, :]) % N) / N)
    kernel = (phase * chirp[None, :]).sum(axis=1) / N
    offset = np.arange(B)[:, None] - np.arange(B)[None, :]
    left, right = [], []
    for k in range(4):
        block = sum((-1j) ** (k * m) * kernel[(offset + B * m) % N] for m in range(4)) / 4.0
        real = np.block([[block.real, -block.imag], [block.imag, block.real]])
        left.append(real)
        right.append(real.T)
    to = lambda x: jnp.asarray(np.stack(x).astype(np.float32)).astype(BF16)
    return to(left), to(right)


def add(x, y):
    return (x[0] + y[0], x[1] + y[1])


def sub(x, y):
    return (x[0] - y[0], x[1] - y[1])


def turned(x, y):
    return (x[0] - y[1], x[1] + y[0])


def turned_back(x, y):
    return (x[0] + y[1], x[1] - y[0])


def dft4(x):
    a, b, c, d = add(x[0], x[2]), sub(x[0], x[2]), add(x[1], x[3]), sub(x[1], x[3])
    return [add(a, c), turned_back(b, d), sub(a, c), turned(b, d)]


def idft4(x):
    a, b, c, d = add(x[0], x[2]), sub(x[0], x[2]), add(x[1], x[3]), sub(x[1], x[3])
    return [add(a, c), turned(b, d), sub(a, c), turned_back(b, d)]


def both_ways(grid, transform):
    grid = [transform(row) for row in grid]
    cols = [transform([grid[k][l] for k in range(4)]) for l in range(4)]
    return [[cols[l][k] for l in range(4)] for k in range(4)]


def mul(x, y):
    return (x[0] * y[0] - x[1] * y[1], x[0] * y[1] + x[1] * y[0])


def dot(a, b):
    return jnp.dot(a, b, preferred_element_type=F32)


def lanes(l):
    return slice(l * B, (l + 1) * B)


def half_angle_tangent(phase):
    x = 0.5 * phase
    y = x * x
    sine, cosine = 0.0, 0.0
    for n in reversed(range(7)):
        sine = sine * y + (-1) ** n / math.factorial(2 * n + 1)
        cosine = cosine * y + (-1) ** n / math.factorial(2 * n)
    return x * sine / cosine


def hermite_tables(psi):
    t = (lax.broadcasted_iota(jnp.int32, (8, N), 1).astype(F32) - (N - 1) / 2.0) / (N / 48.0)
    previous = math.pow(math.pi, -0.25) * jnp.exp(-0.5 * t * t)
    current = math.sqrt(2.0) * t * previous
    psi[0] = previous
    psi[1] = current
    for n in range(1, ORDERS - 1):
        higher = math.sqrt(2.0 / (n + 1.0)) * t * current - math.sqrt(n / (n + 1.0)) * previous
        psi[n + 1] = higher
        previous, current = current, higher


def spot_profile(index, shape, dim):
    coords = lax.broadcasted_iota(jnp.int32, shape, dim).astype(F32) - (N - 1) / 2.0
    centre = index.astype(F32) - (SPOT_SIDE - 1) / 2.0
    offset = (coords - (N / 40.0) * centre) / (N / 120.0)
    return jnp.exp(-offset * offset)


def split(x):
    high = x.astype(BF16)
    return high, (x - high.astype(F32)).astype(BF16)


def main_kernel(
    plane_id, core_id, orders, spots, tan_own, half_own, half_other, left, right, keep, send,
    psi, source_x, far_x, x_ref, v_ref, y_ref, g_ref, mask_ref, tan_ref, grad, sems,
):
    mode, core = plane_id[0], core_id[0]
    arrivals = [pltpu.make_async_copy(tan_own, tan_ref.at[0], sems.at[0])]
    for j in range(1, PLANES):
        for n, (half, at) in enumerate(((half_own, core), (half_other, 1 - core))):
            arrivals.append(
                pltpu.make_async_copy(half.at[:, j - 1], tan_ref.at[j, at], sems.at[2 * j + n - 1])
            )
    for copy in arrivals:
        copy.start()
    hermite_tables(psi)
    source_y = psi[orders[1, mode]]
    row = AMPLITUDE * psi[orders[0, mode]][0:1]
    for k in range(4):
        source_x[k * B : (k + 1) * B, :] = jnp.broadcast_to(row[:, lanes(k)], (B, B)).T

    spot = spots[mode]
    down = spot_profile(spot // SPOT_SIDE, (N, B), 0)
    zero = jnp.zeros((B, B), F32)
    spread = dft4([(down[k * B : (k + 1) * B], zero) for k in range(4)])
    moved = []
    for k in range(4):
        high, low = split(jnp.concatenate(spread[k], axis=0))
        both = dot(left[k], jnp.concatenate([high, low], axis=1))
        total = both[:, :B] + both[:, B:]
        moved.append((total[:B], total[B:]))
    for k, part in enumerate(idft4(moved)):
        far_x[0, k * B : (k + 1) * B, :] = part[0]
        far_x[1, k * B : (k + 1) * B, :] = part[1]
    along = spot_profile(spot % SPOT_SIDE, (8, N), 1)
    zero = jnp.zeros((8, B), F32)
    spread = dft4([(along[:, lanes(l)], zero) for l in range(4)])
    moved = []
    for l in range(4):
        high, low = split(jnp.concatenate(spread[l], axis=1))
        both = dot(jnp.concatenate([high, low], axis=0), right[l])
        total = both[:8] + both[8:]
        moved.append((total[:, :B], total[:, B:]))
    far_y = idft4(moved)

    def rows_of(k, s):
        return pl.ds(k * B + s * STRIP, STRIP)

    def decode(plane, s):
        slot = mode ^ plane
        for k in range(4):
            t = tan_ref[slot, k // 2, (k % 2) * (B // STRIP) + s].astype(F32)
            twice = 2.0 / (1.0 + t * t)
            mask_ref[plane, 0, rows_of(k, s), :] = (twice - 1.0).astype(BF16)
            mask_ref[plane, 1, rows_of(k, s), :] = (twice * t).astype(BF16)

    def mask_at(plane, k, l, s):
        at = mask_ref.at[plane]
        return (at[0, rows_of(k, s), lanes(l)], at[1, rows_of(k, s), lanes(l)])

    def spread_out(grid, s):
        grid = both_ways(grid, dft4)
        for k in range(4):
            for l in range(4):
                x_ref[k, pl.ds(s * STRIP, STRIP), lanes(l)] = grid[k][l][0]
                x_ref[k, pl.ds(B + s * STRIP, STRIP), lanes(l)] = grid[k][l][1]

    def gathered_up(s):
        grid = [
            [(y_ref[l, rows_of(k, s), 0:B], y_ref[l, rows_of(k, s), B : 2 * B]) for l in range(4)]
            for k in range(4)
        ]
        return both_ways(grid, idft4)

    def operate():
        for k in range(4):
            z = dot(left[k], x_ref[k]).astype(BF16)
            for l in range(4):
                v_ref[l, k * B : (k + 1) * B, 0:B] = z[:B, lanes(l)]
                v_ref[l, k * B : (k + 1) * B, B : 2 * B] = z[B:, lanes(l)]
        for l in range(4):
            y_ref[l] = dot(v_ref[l], right[l]).astype(BF16)

    def masked(plane, field, k, l, s):
        g = mul(field, mask_at(plane, k, l, s))
        g_ref[plane, 0, rows_of(k, s), lanes(l)] = g[0]
        g_ref[plane, 1, rows_of(k, s), lanes(l)] = g[1]
        return g

    def first_strip(s, carry):
        decode(0, s)

        def at(k, l):
            field = (source_x[rows_of(k, s), :] * source_y[0:1, lanes(l)]).astype(BF16)
            mask = mask_at(0, k, l, s)
            g = (field * mask[0], field * mask[1])
            g_ref[0, 0, rows_of(k, s), lanes(l)] = g[0]
            g_ref[0, 1, rows_of(k, s), lanes(l)] = g[1]
            return g

        spread_out([[at(k, l) for l in range(4)] for k in range(4)], s)
        return carry

    def forward_strip(plane, s, carry):
        decode(plane, s)
        field = gathered_up(s)
        spread_out([[masked(plane, field[k][l], k, l, s) for l in range(4)] for k in range(4)], s)
        return carry

    def last_strip(s, carry):
        decode(PLANES - 1, s)
        field = gathered_up(s)
        carry = list(carry)
        for k in range(4):
            a = (far_x[0, rows_of(k, s), :], far_x[1, rows_of(k, s), :])
            for l in range(4):
                g = masked(PLANES - 1, field[k][l], k, l, s)
                carry[l] = add(carry[l], mul((g[0].astype(F32), g[1].astype(F32)), a))
        return tuple(carry)

    def returned(plane, back, k, l, s):
        g = (g_ref[plane, 0, rows_of(k, s), lanes(l)], g_ref[plane, 1, rows_of(k, s), lanes(l)])
        piece = 2 * ((k % 2) * (B // STRIP) + s) + l // 2
        grad[k // 2, piece, mode ^ plane, :, lanes(l % 2)] = back[0] * g[1] + back[1] * g[0]
        return mul(back, mask_at(plane, k, l, s)) if plane else None

    strips = B // STRIP
    for copy in arrivals:
        copy.wait()
    lax.fori_loop(0, strips, first_strip, 0)
    for plane in range(1, PLANES - 1):
        operate()
        lax.fori_loop(0, strips, functools.partial(forward_strip, plane), 0)
    operate()
    nothing = jnp.zeros((STRIP, B), F32)
    sums = lax.fori_loop(0, strips, last_strip, tuple((nothing, nothing) for _ in range(4)))
    total = [mul((s[0][:8] + s[0][8:], s[1][:8] + s[1][8:]), y) for s, y in zip(sums, far_y)]
    coupling_re = jnp.sum(sum(t[0] for t in total))
    coupling_im = jnp.sum(sum(t[1] for t in total))
    back_y = [
        (
            (coupling_re * y[0] + coupling_im * y[1])[0:1],
            (coupling_re * y[1] - coupling_im * y[0])[0:1],
        )
        for y in far_y
    ]

    def turn_strip(s, carry):
        def at(k, l):
            a = (far_x[0, rows_of(k, s), :], far_x[1, rows_of(k, s), :])
            back = mul(a, back_y[l])
            return returned(PLANES - 1, (back[0].astype(BF16), back[1].astype(BF16)), k, l, s)

        spread_out([[at(k, l) for l in range(4)] for k in range(4)], s)
        return carry

    def backward_strip(plane, s, carry):
        back = gathered_up(s)
        reply = [[returned(plane, back[k][l], k, l, s) for l in range(4)] for k in range(4)]
        if plane:
            spread_out(reply, s)
        return carry

    lax.fori_loop(0, strips, turn_strip, 0)
    for plane in reversed(range(PLANES - 1)):
        operate()
        lax.fori_loop(0, strips, functools.partial(backward_strip, plane), 0)
    departures = [
        pltpu.make_async_copy(grad.at[1 - core], send, sems.at[0]),
        pltpu.make_async_copy(grad.at[core], keep, sems.at[1]),
    ]
    for copy in departures:
        copy.start()
    for copy in departures:
        copy.wait()


def main_call(plane_id, core_id, orders, spots, tan_own, half_own, half_other, left, right):
    pieces = (2 * HALF_STRIPS, PLANES, STRIP, N // 2)
    return pl.pallas_call(
        main_kernel,
        name="modes",
        in_specs=[SMEM, SMEM, SMEM, SMEM, ANY, ANY, ANY, VMEM, VMEM],
        out_specs=[ANY, ANY],
        out_shape=[jax.ShapeDtypeStruct(pieces, BF16)] * 2,
        scratch_shapes=[
            pltpu.VMEM((ORDERS, 8, N), F32),
            pltpu.VMEM((N, B), F32),
            pltpu.VMEM((2, N, B), F32),
            pltpu.VMEM((4, 2 * B, N), BF16),
            pltpu.VMEM((4, N, 2 * B), BF16),
            pltpu.VMEM((4, N, 2 * B), BF16),
            pltpu.VMEM((PLANES, 2, N, N), BF16),
            pltpu.VMEM((PLANES, 2, N, N), BF16),
            pltpu.VMEM((PLANES, 2, HALF_STRIPS, STRIP, N), BF16),
            pltpu.VMEM((2, *pieces), BF16),
            pltpu.SemaphoreType.DMA((7,)),
        ],
        compiler_params=vmem_limit(26),
    )(plane_id, core_id, orders, spots, tan_own, half_own, half_other, left, right)


def tangent_kernel(where, phase, out, rows, sem):
    copy = pltpu.make_async_copy(phase.at[0, pl.ds(where[0] * STRIP, STRIP)], rows, sem)
    copy.start()
    copy.wait()
    out[...] = half_angle_tangent(rows[...]).astype(BF16)


def tangent_call(where, phase_masks):
    return pl.pallas_call(
        tangent_kernel,
        name="tangent",
        in_specs=[SMEM, pl.BlockSpec(memory_space=pltpu.HBM)],
        out_specs=VMEM,
        out_shape=jax.ShapeDtypeStruct((STRIP, N), BF16),
        scratch_shapes=[pltpu.VMEM((STRIP, N), F32), pltpu.SemaphoreType.DMA],
        compiler_params=vmem_limit(4),
    )(where, phase_masks)


def own_tangent_kernel(phase, out):
    def strip(i, carry):
        x = phase[0, pl.ds(i * STRIP, STRIP), :]
        out[i // HALF_STRIPS, i % HALF_STRIPS] = half_angle_tangent(x).astype(BF16)
        return carry

    lax.fori_loop(0, N // STRIP, strip, 0)


def own_tangent_call(phase_masks):
    return pl.pallas_call(
        own_tangent_kernel,
        name="own_tangent",
        in_specs=[VMEM],
        out_specs=VMEM,
        out_shape=jax.ShapeDtypeStruct((2, HALF_STRIPS, STRIP, N), BF16),
        compiler_params=vmem_limit(6),
    )(phase_masks)


def finish_kernel(core_id, phase, own, other, out):
    squares = jnp.zeros((STRIP, N // 2), F32)
    for piece in range(2 * HALF_STRIPS):
        for part in (own, other):
            x = part[piece].astype(F32)
            squares += x * x
    mean = 4.0 * jnp.sum(squares, keepdims=True) / (N * N)
    scale = -2.0 * lax.rsqrt(mean + EPSILON)
    core = core_id[0]
    for part, half in ((own, core), (other, 1 - core)):
        for piece in range(2 * HALF_STRIPS):
            rows = pl.ds(half * (N // 2) + (piece // 2) * STRIP, STRIP)
            cols = slice((piece % 2) * (N // 2), (piece % 2 + 1) * (N // 2))
            out[0, rows, cols] = phase[0, rows, cols] + part[piece].astype(F32) * scale


def finish_call(core_id, phase_masks, own, other):
    return pl.pallas_call(
        finish_kernel,
        name="finish",
        in_specs=[SMEM, VMEM, VMEM, VMEM],
        out_specs=VMEM,
        out_shape=jax.ShapeDtypeStruct((1, N, N), F32),
        compiler_params=vmem_limit(8),
    )(core_id, phase_masks, own, other)


def swapped(x):
    return lax.ppermute(x, CORE, [(0, 1), (1, 0)])


def from_plane(x, step):
    return lax.ppermute(x, "plane", [(p, p ^ step) for p in range(PLANES)])


def exchanged(x, axes):
    return lax.all_to_all(x, axes, split_axis=0, concat_axis=0, tiled=True)


def from_everyone(x, axes):
    count = lax.axis_size(axes)
    return exchanged(jnp.broadcast_to(x[None], (count, *x.shape)), axes)


def shards(phase_masks, hg_orders, spot_index):
    core = lax.axis_index(CORE).astype(jnp.int32)
    plane_id, core_id = lax.axis_index("plane").astype(jnp.int32)[None], core[None]
    group = core * XY_DEVICES + lax.axis_index(XY).astype(jnp.int32)
    tangent = tangent_call(group[None], phase_masks)
    tan_own = own_tangent_call(phase_masks)
    near = from_plane(tangent, 1)
    far = from_plane(jnp.stack([tangent, near]), 2)
    half_own = from_everyone(jnp.concatenate([near[None], far]), XY)
    half_other = swapped(half_own)
    left, right = block_operators()
    keep, send = main_call(
        plane_id, core_id, hg_orders.T, spot_index, tan_own, half_own, half_other, left, right
    )
    pair = keep + swapped(send)
    column = jnp.sum(exchanged(pair, CHIPS).astype(F32), axis=0).astype(BF16)
    two = column[:2] + from_plane(column[2:], 2)
    total = two[0] + from_plane(two[1], 1)
    own = from_everyone(total, CHIPS)
    other = swapped(own)
    return finish_call(core_id, phase_masks, own, other)


def solution(mesh):
    finer = Mesh(
        mesh.devices.reshape(mesh.shape["plane"], 4, 4, 2, 2),
        ("plane", "mode_0", "mode_1", "mode_2", "mode_3"),
    )
    placed = (P("plane", None, None), P(MODE, None), P(MODE))
    return jax.shard_map(
        shards, mesh=finer, in_specs=placed, out_specs=P("plane", None, None), check_vma=False
    )
```

```python
import functools
import math

import jax
import jax.numpy as jnp
import numpy as np
from jax import lax
from jax.experimental import pallas as pl
from jax.experimental.pallas import tpu as pltpu
from jax.sharding import Mesh
from jax.sharding import PartitionSpec as P

ORDERS = 45
SPOT_SIDE = 32
MODE = ("mode_0", "mode_1", "mode_2", "mode_3")
XY = ("mode_0", "mode_1")
CHIPS = ("mode_0", "mode_1", "mode_2")
ALL_CHIPS = ("plane", *CHIPS)
CORE = "mode_3"
PLANES = 4
N = 512
B = 128
STRIP = 16
HALF_STRIPS = N // STRIP // 2
PIECE = (STRIP, N // 2)
PIECES = 2 * HALF_STRIPS
CHIRP_RATE = math.pi / 48.0 * (math.pi / 48.0)
AMPLITUDE = 12.0
EPSILON = 1e-06
F32 = jnp.float32
BF16 = jnp.bfloat16
SMEM = pl.BlockSpec(memory_space=pltpu.SMEM)
VMEM = pl.BlockSpec(memory_space=pltpu.VMEM)
ANY = pl.BlockSpec(memory_space=pl.ANY)
HBM = pl.BlockSpec(memory_space=pltpu.HBM)


def vmem_limit(mib):
    return pltpu.CompilerParams(vmem_limit_bytes=mib << 20)


def block_operators():
    f = np.arange(N)
    s = (f + N // 2) % N - N // 2
    chirp = np.exp(-1j * CHIRP_RATE * s.astype(np.float64) ** 2)
    phase = np.exp(2j * np.pi * ((f[:, None] * f[None, :]) % N) / N)
    kernel = (phase * chirp[None, :]).sum(axis=1) / N
    offset = np.arange(B)[:, None] - np.arange(B)[None, :]
    left, right = [], []
    for k in range(4):
        block = sum((-1j) ** (k * m) * kernel[(offset + B * m) % N] for m in range(4)) / 4.0
        real = np.block([[block.real, -block.imag], [block.imag, block.real]])
        left.append(real)
        right.append(real.T)
    to = lambda x: jnp.asarray(np.stack(x).astype(np.float32)).astype(BF16)
    return to(left), to(right)


def add(x, y):
    return (x[0] + y[0], x[1] + y[1])


def sub(x, y):
    return (x[0] - y[0], x[1] - y[1])


def turned(x, y):
    return (x[0] - y[1], x[1] + y[0])


def turned_back(x, y):
    return (x[0] + y[1], x[1] - y[0])


def dft4(x):
    a, b, c, d = add(x[0], x[2]), sub(x[0], x[2]), add(x[1], x[3]), sub(x[1], x[3])
    return [add(a, c), turned_back(b, d), sub(a, c), turned(b, d)]


def idft4(x):
    a, b, c, d = add(x[0], x[2]), sub(x[0], x[2]), add(x[1], x[3]), sub(x[1], x[3])
    return [add(a, c), turned(b, d), sub(a, c), turned_back(b, d)]


def both_ways(grid, transform):
    grid = [transform(row) for row in grid]
    cols = [transform([grid[k][l] for k in range(4)]) for l in range(4)]
    return [[cols[l][k] for l in range(4)] for k in range(4)]


def mul(x, y):
    return (x[0] * y[0] - x[1] * y[1], x[0] * y[1] + x[1] * y[0])


def dot(a, b):
    return jnp.dot(a, b, preferred_element_type=F32)


def lanes(l):
    return slice(l * B, (l + 1) * B)


def half_angle_tangent(phase):
    x = 0.5 * phase
    y = x * x
    sine, cosine = 0.0, 0.0
    for n in reversed(range(7)):
        sine = sine * y + (-1) ** n / math.factorial(2 * n + 1)
        cosine = cosine * y + (-1) ** n / math.factorial(2 * n)
    return x * sine / cosine


def hermite_tables(psi):
    t = (lax.broadcasted_iota(jnp.int32, (8, N), 1).astype(F32) - (N - 1) / 2.0) / (N / 48.0)
    previous = math.pow(math.pi, -0.25) * jnp.exp(-0.5 * t * t)
    current = math.sqrt(2.0) * t * previous
    psi[0] = previous
    psi[1] = current
    for n in range(1, ORDERS - 1):
        higher = math.sqrt(2.0 / (n + 1.0)) * t * current - math.sqrt(n / (n + 1.0)) * previous
        psi[n + 1] = higher
        previous, current = current, higher


def spot_profile(index, shape, dim):
    coords = lax.broadcasted_iota(jnp.int32, shape, dim).astype(F32) - (N - 1) / 2.0
    centre = index.astype(F32) - (SPOT_SIDE - 1) / 2.0
    offset = (coords - (N / 40.0) * centre) / (N / 120.0)
    return jnp.exp(-offset * offset)


def split(x):
    high = x.astype(BF16)
    return high, (x - high.astype(F32)).astype(BF16)


def main_kernel(
    plane_id, core_id, orders_in, spots_in, half_own, half_other, left_in, right_in, keep, send,
    orders, spots, left, right, psi, source_x, far_x, x_ref, v_ref, y_ref, g_ref, mask_ref, tan_ref, grad, sems,
):
    mode, core = plane_id[0], core_id[0]
    pairs = (
        (orders_in, orders),
        (spots_in, spots),
        (left_in, left),
        (right_in, right),
        (half_own, tan_ref.at[core]),
        (half_other, tan_ref.at[1 - core]),
    )
    arrivals = [pltpu.make_async_copy(*pair, sems.at[n]) for n, pair in enumerate(pairs)]
    for copy in arrivals:
        copy.start()
    for copy in arrivals[:2]:
        copy.wait()
    hermite_tables(psi)
    source_y = psi[orders[1, mode]]
    row = AMPLITUDE * psi[orders[0, mode]][0:1]
    for k in range(4):
        source_x[k * B : (k + 1) * B, :] = jnp.broadcast_to(row[:, lanes(k)], (B, B)).T

    for copy in arrivals[2:4]:
        copy.wait()
    spot = spots[mode]
    down = spot_profile(spot // SPOT_SIDE, (N, B), 0)
    zero = jnp.zeros((B, B), F32)
    spread = dft4([(down[k * B : (k + 1) * B], zero) for k in range(4)])
    moved = []
    for k in range(4):
        high, low = split(jnp.concatenate(spread[k], axis=0))
        both = dot(left[k], jnp.concatenate([high, low], axis=1))
        total = both[:, :B] + both[:, B:]
        moved.append((total[:B], total[B:]))
    for k, part in enumerate(idft4(moved)):
        far_x[0, k * B : (k + 1) * B, :] = part[0]
        far_x[1, k * B : (k + 1) * B, :] = part[1]
    along = spot_profile(spot % SPOT_SIDE, (8, N), 1)
    zero = jnp.zeros((8, B), F32)
    spread = dft4([(along[:, lanes(l)], zero) for l in range(4)])
    moved = []
    for l in range(4):
        high, low = split(jnp.concatenate(spread[l], axis=1))
        both = dot(jnp.concatenate([high, low], axis=0), right[l])
        total = both[:8] + both[8:]
        moved.append((total[:, :B], total[:, B:]))
    far_y = idft4(moved)

    def rows_of(k, s):
        return pl.ds(k * B + s * STRIP, STRIP)

    def decode(plane, s):
        for k in range(4):
            for h in range(2):
                cols = slice(h * 2 * B, (h + 1) * 2 * B)
                t = tan_ref[k // 2, plane, 2 * ((k % 2) * (B // STRIP) + s) + h].astype(F32)
                twice = 2.0 / (1.0 + t * t)
                mask_ref[plane, 0, rows_of(k, s), cols] = (twice - 1.0).astype(BF16)
                mask_ref[plane, 1, rows_of(k, s), cols] = (twice * t).astype(BF16)

    def mask_at(plane, k, l, s):
        at = mask_ref.at[plane]
        return (at[0, rows_of(k, s), lanes(l)], at[1, rows_of(k, s), lanes(l)])

    def spread_out(grid, s):
        grid = both_ways(grid, dft4)
        for k in range(4):
            for l in range(4):
                x_ref[k, pl.ds(s * STRIP, STRIP), lanes(l)] = grid[k][l][0]
                x_ref[k, pl.ds(B + s * STRIP, STRIP), lanes(l)] = grid[k][l][1]

    def gathered_up(s):
        grid = [
            [(y_ref[l, rows_of(k, s), 0:B], y_ref[l, rows_of(k, s), B : 2 * B]) for l in range(4)]
            for k in range(4)
        ]
        return both_ways(grid, idft4)

    def operate():
        for k in range(4):
            z = dot(left[k], x_ref[k]).astype(BF16)
            for l in range(4):
                v_ref[l, k * B : (k + 1) * B, 0:B] = z[:B, lanes(l)]
                v_ref[l, k * B : (k + 1) * B, B : 2 * B] = z[B:, lanes(l)]
        for l in range(4):
            y_ref[l] = dot(v_ref[l], right[l]).astype(BF16)

    def masked(plane, field, k, l, s):
        g = mul(field, mask_at(plane, k, l, s))
        g_ref[plane, 0, rows_of(k, s), lanes(l)] = g[0]
        g_ref[plane, 1, rows_of(k, s), lanes(l)] = g[1]
        return g

    def first_strip(s, carry):
        decode(0, s)

        def at(k, l):
            field = (source_x[rows_of(k, s), :] * source_y[0:1, lanes(l)]).astype(BF16)
            mask = mask_at(0, k, l, s)
            g = (field * mask[0], field * mask[1])
            g_ref[0, 0, rows_of(k, s), lanes(l)] = g[0]
            g_ref[0, 1, rows_of(k, s), lanes(l)] = g[1]
            return g

        spread_out([[at(k, l) for l in range(4)] for k in range(4)], s)
        return carry

    def forward_strip(plane, s, carry):
        decode(plane, s)
        field = gathered_up(s)
        spread_out([[masked(plane, field[k][l], k, l, s) for l in range(4)] for k in range(4)], s)
        return carry

    def last_strip(s, carry):
        decode(PLANES - 1, s)
        field = gathered_up(s)
        carry = list(carry)
        for k in range(4):
            a = (far_x[0, rows_of(k, s), :], far_x[1, rows_of(k, s), :])
            for l in range(4):
                g = masked(PLANES - 1, field[k][l], k, l, s)
                carry[l] = add(carry[l], mul((g[0].astype(F32), g[1].astype(F32)), a))
        return tuple(carry)

    def returned(plane, back, k, l, s):
        g = (g_ref[plane, 0, rows_of(k, s), lanes(l)], g_ref[plane, 1, rows_of(k, s), lanes(l)])
        piece = 2 * ((k % 2) * (B // STRIP) + s) + l // 2
        grad[k // 2, plane, piece, :, lanes(l % 2)] = back[0] * g[1] + back[1] * g[0]
        return mul(back, mask_at(plane, k, l, s)) if plane else None

    strips = B // STRIP
    for copy in arrivals[4:]:
        copy.wait()
    lax.fori_loop(0, strips, first_strip, 0)
    for plane in range(1, PLANES - 1):
        operate()
        lax.fori_loop(0, strips, functools.partial(forward_strip, plane), 0)
    operate()
    nothing = jnp.zeros((STRIP, B), F32)
    sums = lax.fori_loop(0, strips, last_strip, tuple((nothing, nothing) for _ in range(4)))
    total = [mul((s[0][:8] + s[0][8:], s[1][:8] + s[1][8:]), y) for s, y in zip(sums, far_y)]
    coupling_re = jnp.sum(sum(t[0] for t in total))
    coupling_im = jnp.sum(sum(t[1] for t in total))
    back_y = [
        (
            (coupling_re * y[0] + coupling_im * y[1])[0:1],
            (coupling_re * y[1] - coupling_im * y[0])[0:1],
        )
        for y in far_y
    ]

    def turn_strip(s, carry):
        def at(k, l):
            a = (far_x[0, rows_of(k, s), :], far_x[1, rows_of(k, s), :])
            back = mul(a, back_y[l])
            return returned(PLANES - 1, (back[0].astype(BF16), back[1].astype(BF16)), k, l, s)

        spread_out([[at(k, l) for l in range(4)] for k in range(4)], s)
        return carry

    def backward_strip(plane, s, carry):
        back = gathered_up(s)
        reply = [[returned(plane, back[k][l], k, l, s) for l in range(4)] for k in range(4)]
        if plane:
            spread_out(reply, s)
        return carry

    lax.fori_loop(0, strips, turn_strip, 0)
    for plane in reversed(range(PLANES - 1)):
        operate()
        lax.fori_loop(0, strips, functools.partial(backward_strip, plane), 0)
    departures = [
        pltpu.make_async_copy(grad.at[1 - core], send, sems.at[0]),
        pltpu.make_async_copy(grad.at[core], keep, sems.at[1]),
    ]
    for copy in departures:
        copy.start()
    for copy in departures:
        copy.wait()


def main_call(plane_id, core_id, orders, spots, half_own, half_other, left, right):
    half = (PLANES, PIECES, *PIECE)
    return pl.pallas_call(
        main_kernel,
        name="modes",
        in_specs=[SMEM, SMEM, HBM, HBM, ANY, ANY, HBM, HBM],
        out_specs=[ANY, ANY],
        out_shape=[jax.ShapeDtypeStruct(half, BF16)] * 2,
        scratch_shapes=[
            pltpu.SMEM((2, PLANES), jnp.int32),
            pltpu.SMEM((PLANES,), jnp.int32),
            pltpu.VMEM((4, 2 * B, 2 * B), BF16),
            pltpu.VMEM((4, 2 * B, 2 * B), BF16),
            pltpu.VMEM((ORDERS, 8, N), F32),
            pltpu.VMEM((N, B), F32),
            pltpu.VMEM((2, N, B), F32),
            pltpu.VMEM((4, 2 * B, N), BF16),
            pltpu.VMEM((4, N, 2 * B), BF16),
            pltpu.VMEM((4, N, 2 * B), BF16),
            pltpu.VMEM((PLANES, 2, N, N), BF16),
            pltpu.VMEM((PLANES, 2, N, N), BF16),
            pltpu.VMEM((2, *half), BF16),
            pltpu.VMEM((2, *half), BF16),
            pltpu.SemaphoreType.DMA((6,)),
        ],
        compiler_params=vmem_limit(26),
    )(plane_id, core_id, orders, spots, half_own, half_other, left, right)


def tangent_kernel(strip_id, side_id, phase, out, rows, sem):
    for side in range(2):

        @pl.when(side_id[0] == side)
        def _():
            at = phase.at[0, pl.ds(strip_id[0] * STRIP, STRIP), side * (N // 2) : (side + 1) * (N // 2)]
            copy = pltpu.make_async_copy(at, rows, sem)
            copy.start()
            copy.wait()

    out[...] = half_angle_tangent(rows[...]).astype(BF16)


def tangent_call(strip_id, side_id, phase_masks):
    return pl.pallas_call(
        tangent_kernel,
        name="tangent",
        in_specs=[SMEM, SMEM, HBM],
        out_specs=VMEM,
        out_shape=jax.ShapeDtypeStruct(PIECE, BF16),
        scratch_shapes=[pltpu.VMEM(PIECE, F32), pltpu.SemaphoreType.DMA],
        compiler_params=vmem_limit(59),
    )(strip_id, side_id, phase_masks)


def finish_kernel(core_id, phase_in, own, other, out, phase, sem):
    arrival = pltpu.make_async_copy(phase_in, phase, sem)
    arrival.start()
    squares = jnp.zeros(PIECE, F32)
    for piece in range(PIECES):
        for part in (own, other):
            x = part[piece].astype(F32)
            squares += x * x
    mean = 4.0 * jnp.sum(squares, keepdims=True) / (N * N)
    scale = -2.0 * lax.rsqrt(mean + EPSILON)
    core = core_id[0]
    arrival.wait()
    for part, half in ((own, core), (other, 1 - core)):
        for piece in range(PIECES):
            rows = pl.ds(half * (N // 2) + (piece // 2) * STRIP, STRIP)
            cols = slice((piece % 2) * (N // 2), (piece % 2 + 1) * (N // 2))
            out[0, rows, cols] = phase[0, rows, cols] + part[piece].astype(F32) * scale


def finish_call(core_id, phase_masks, own, other):
    return pl.pallas_call(
        finish_kernel,
        name="finish",
        in_specs=[SMEM, HBM, VMEM, VMEM],
        out_specs=VMEM,
        out_shape=jax.ShapeDtypeStruct((1, N, N), F32),
        scratch_shapes=[pltpu.VMEM((1, N, N), F32), pltpu.SemaphoreType.DMA],
        compiler_params=vmem_limit(8),
    )(core_id, phase_masks, own, other)


def swapped(x):
    return lax.ppermute(x, CORE, [(0, 1), (1, 0)])


def exchanged(x, axes):
    return lax.all_to_all(x, axes, split_axis=0, concat_axis=0, tiled=True)


def from_everyone(x, axes):
    count = lax.axis_size(axes)
    return exchanged(jnp.broadcast_to(x[None], (count, *x.shape)), axes)


def shards(phase_masks, hg_orders, spot_index):
    core = lax.axis_index(CORE).astype(jnp.int32)
    plane_id, core_id = lax.axis_index("plane").astype(jnp.int32)[None], core[None]
    strip_id = (core * HALF_STRIPS + lax.axis_index(XY).astype(jnp.int32))[None]
    side_id = lax.axis_index("mode_2").astype(jnp.int32)[None]
    half = (PLANES, PIECES, *PIECE)
    half_own = from_everyone(tangent_call(strip_id, side_id, phase_masks), ALL_CHIPS).reshape(half)
    half_other = swapped(half_own)
    left, right = block_operators()
    keep, send = main_call(
        plane_id, core_id, hg_orders.T, spot_index, half_own, half_other, left, right
    )
    pair = (keep + swapped(send)).reshape(PLANES * PIECES, *PIECE)
    total = jnp.sum(exchanged(pair, ALL_CHIPS).astype(F32), axis=0).astype(BF16)
    own = from_everyone(total, CHIPS)
    other = swapped(own)
    return finish_call(core_id, phase_masks, own, other)


def solution(mesh):
    finer = Mesh(
        mesh.devices.reshape(mesh.shape["plane"], 4, 4, 2, 2),
        ("plane", "mode_0", "mode_1", "mode_2", "mode_3"),
    )
    placed = (P("plane", None, None), P(MODE, None), P(MODE))
    return jax.shard_map(
        shards, mesh=finer, in_specs=placed, out_specs=P("plane", None, None), check_vma=False
    )
```

```python
import functools
import math

import jax
import jax.numpy as jnp
import numpy as np
from jax import lax
from jax.experimental import pallas as pl
from jax.experimental.pallas import tpu as pltpu
from jax.sharding import Mesh
from jax.sharding import PartitionSpec as P

ORDERS = 45
SPOT_SIDE = 32
MODE = ("mode_0", "mode_1", "mode_2", "mode_3")
XY = ("mode_0", "mode_1")
Z = ("plane", "mode_2")
CORE = "mode_3"
PLANES = 4
N = 512
B = 128
U = B // 2
W = 2 * B
WIDE = 4 * W
STRIP = 8
STRIPS = U // STRIP
CHUNKS = 4
PIECE = (16, W)
GROUPS = 8
CHIRP_RATE = math.pi / 48.0 * (math.pi / 48.0)
AMPLITUDE = 12.0
EPSILON = 1e-06
F32 = jnp.float32
BF16 = jnp.bfloat16
SMEM = pl.BlockSpec(memory_space=pltpu.SMEM)
VMEM = pl.BlockSpec(memory_space=pltpu.VMEM)
ANY = pl.BlockSpec(memory_space=pl.ANY)
HBM = pl.BlockSpec(memory_space=pltpu.HBM)


def vmem_limit(mib):
    return pltpu.CompilerParams(vmem_limit_bytes=mib << 20)


def block_operators():
    f = np.arange(N)
    s = (f + N // 2) % N - N // 2
    chirp = np.exp(-1j * CHIRP_RATE * s.astype(np.float64) ** 2)
    phase = np.exp(2j * np.pi * ((f[:, None] * f[None, :]) % N) / N)
    kernel = (phase * chirp[None, :]).sum(axis=1) / N
    offset = np.arange(B)[:, None] - np.arange(B)[None, :]
    left, right = [], []
    for k in range(4):
        block = sum((-1j) ** (k * m) * kernel[(offset + B * m) % N] for m in range(4)) / 4.0
        real = np.block([[block.real, -block.imag], [block.imag, block.real]])
        left.append(real)
        right.append(real.T)
    to = lambda x: jnp.asarray(np.stack(x).astype(np.float32)).astype(BF16)
    return to(left), to(right)


def add(x, y):
    return (x[0] + y[0], x[1] + y[1])


def sub(x, y):
    return (x[0] - y[0], x[1] - y[1])


def turned(x, y):
    return (x[0] - y[1], x[1] + y[0])


def turned_back(x, y):
    return (x[0] + y[1], x[1] - y[0])


def dft4(x):
    a, b, c, d = add(x[0], x[2]), sub(x[0], x[2]), add(x[1], x[3]), sub(x[1], x[3])
    return [add(a, c), turned_back(b, d), sub(a, c), turned(b, d)]


def idft4(x):
    a, b, c, d = add(x[0], x[2]), sub(x[0], x[2]), add(x[1], x[3]), sub(x[1], x[3])
    return [add(a, c), turned(b, d), sub(a, c), turned_back(b, d)]


def both_ways(grid, transform):
    grid = [transform(row) for row in grid]
    cols = [transform([grid[k][l] for k in range(4)]) for l in range(4)]
    return [[cols[l][k] for l in range(4)] for k in range(4)]


def mul(x, y):
    return (x[0] * y[0] - x[1] * y[1], x[0] * y[1] + x[1] * y[0])


def dot(a, b):
    return jnp.dot(a, b, preferred_element_type=F32)


def lanes(l):
    return slice(l * B, (l + 1) * B)


def half_angle_tangent(phase):
    x = 0.5 * phase
    y = x * x
    sine, cosine = 0.0, 0.0
    for n in reversed(range(7)):
        sine = sine * y + (-1) ** n / math.factorial(2 * n + 1)
        cosine = cosine * y + (-1) ** n / math.factorial(2 * n)
    return x * sine / cosine


def hermite_tables(psi):
    t = (lax.broadcasted_iota(jnp.int32, (8, N), 1).astype(F32) - (N - 1) / 2.0) / (N / 48.0)
    previous = math.pow(math.pi, -0.25) * jnp.exp(-0.5 * t * t)
    current = math.sqrt(2.0) * t * previous
    psi[0] = previous
    psi[1] = current
    for n in range(1, ORDERS - 1):
        higher = math.sqrt(2.0 / (n + 1.0)) * t * current - math.sqrt(n / (n + 1.0)) * previous
        psi[n + 1] = higher
        previous, current = current, higher


def spot_profile(index, shape, dim):
    coords = lax.broadcasted_iota(jnp.int32, shape, dim).astype(F32) - (N - 1) / 2.0
    centre = index.astype(F32) - (SPOT_SIDE - 1) / 2.0
    offset = (coords - (N / 40.0) * centre) / (N / 120.0)
    return jnp.exp(-offset * offset)


def split(x):
    high = x.astype(BF16)
    return high, (x - high.astype(F32)).astype(BF16)


def wide(l):
    return slice(l * W, (l + 1) * W)


def beside(x):
    return jnp.concatenate([x[:U], x[U:]], axis=1)


def setup_kernel(plane_id, orders_in, spots_in, left_in, right_in, left, right, source_x, source_y, far_x, far_y,
                 orders, spots, psi, sems):
    mode = plane_id[0]
    pairs = [(orders_in, orders), (spots_in, spots), (left_in, left), (right_in, right)]
    arrivals = [pltpu.make_async_copy(*pair, sems.at[n]) for n, pair in enumerate(pairs)]
    for copy in arrivals:
        copy.start()
    for copy in arrivals[:2]:
        copy.wait()
    hermite_tables(psi)
    row = psi[orders[1, mode]]
    for l in range(4):
        source_y[l] = jnp.concatenate([row[:, lanes(l)]] * 2, axis=1)
    row = AMPLITUDE * psi[orders[0, mode]][0:1]
    for k in range(4):
        source_x[k] = beside(jnp.broadcast_to(row[:, lanes(k)], (B, B)).T)

    for copy in arrivals[2:]:
        copy.wait()
    spot = spots[mode]
    down = spot_profile(spot // SPOT_SIDE, (N, B), 0)
    zero = jnp.zeros((B, B), F32)
    spread = dft4([(down[k * B : (k + 1) * B], zero) for k in range(4)])
    moved = []
    for k in range(4):
        high, low = split(jnp.concatenate(spread[k], axis=0))
        both = dot(left[k], jnp.concatenate([high, low], axis=1))
        total = both[:, :B] + both[:, B:]
        moved.append((total[:B], total[B:]))
    for k, part in enumerate(idft4(moved)):
        far_x[0, k] = beside(part[0]).astype(BF16)
        far_x[1, k] = beside(part[1]).astype(BF16)
    along = spot_profile(spot % SPOT_SIDE, (8, N), 1)
    zero = jnp.zeros((8, B), F32)
    spread = dft4([(along[:, lanes(l)], zero) for l in range(4)])
    moved = []
    for l in range(4):
        high, low = split(jnp.concatenate(spread[l], axis=1))
        both = dot(jnp.concatenate([high, low], axis=0), right[l])
        total = both[:8] + both[8:]
        moved.append((total[:, :B], total[:, B:]))
    for l, y in enumerate(idft4(moved)):
        for c in range(2):
            far_y[c, l] = jnp.concatenate([y[c]] * 2, axis=1)


def setup_call(plane_id, orders, spots, left, right):
    return pl.pallas_call(
        setup_kernel,
        name="setup",
        in_specs=[SMEM, HBM, HBM, HBM, HBM],
        out_specs=[VMEM] * 6,
        out_shape=[
            jax.ShapeDtypeStruct(left.shape, BF16),
            jax.ShapeDtypeStruct(right.shape, BF16),
            jax.ShapeDtypeStruct((4, U, W), F32),
            jax.ShapeDtypeStruct((4, 8, W), F32),
            jax.ShapeDtypeStruct((2, 4, U, W), BF16),
            jax.ShapeDtypeStruct((2, 4, 8, W), F32),
        ],
        scratch_shapes=[
            pltpu.SMEM((2, PLANES), jnp.int32),
            pltpu.SMEM((PLANES,), jnp.int32),
            pltpu.VMEM((ORDERS, 8, N), F32),
            pltpu.SemaphoreType.DMA((4,)),
        ],
        compiler_params=vmem_limit(8),
    )(plane_id, orders, spots, left, right)


def main_kernel(
    plane_id, core_id, side_id, tan_own, *refs,
):
    tan_in, (left, right, source_x, source_y, far_x, far_y, keep, send) = refs[:6], refs[6:14]
    x_ref, v_ref, y_ref, g_ref, mask_ref, tan_ref, grad, sems = refs[14:]
    mode, core, side = plane_id[0], core_id[0], side_id[0]
    pairs = [(tan_own, tan_ref.at[0])]
    for at, (straight, before, after) in ((core, tan_in[:3]), (1 - core, tan_in[3:])):
        across = slice(1, PLANES)
        pairs.append((straight, tan_ref.at[across, at, side]))
        pairs.append((before, tan_ref.at[across, at, 1 - side, 0 : GROUPS // 2]))
        pairs.append((after, tan_ref.at[across, at, 1 - side, GROUPS // 2 : GROUPS]))
    arrivals = [pltpu.make_async_copy(*pair, sems.at[n]) for n, pair in enumerate(pairs)]
    for copy in arrivals:
        copy.start()

    def rows_of(s):
        return slice(s * STRIP, (s + 1) * STRIP)

    def piece_of(k, s):
        return k // 2, (s // 2) * 2, slice((s % 2) * STRIP, (s % 2 + 1) * STRIP)

    def decode(plane, s):
        for k in range(4):
            half, group, rows = piece_of(k, s)
            for l in range(4):
                t = tan_ref[(plane - mode) & 3, half, k % 2, group + l // 2, l % 2, rows].astype(F32)
                twice = 2.0 / (1.0 + t * t)
                mask_ref[plane, 0, k, rows_of(s), wide(l)] = (twice - 1.0).astype(BF16)
                mask_ref[plane, 1, k, rows_of(s), wide(l)] = (twice * t).astype(BF16)

    def load(ref, k, l, s):
        return (ref[0, k, rows_of(s), wide(l)], ref[1, k, rows_of(s), wide(l)])

    def store(ref, k, l, s, x):
        ref[0, k, rows_of(s), wide(l)] = x[0]
        ref[1, k, rows_of(s), wide(l)] = x[1]

    def spread_out(grid, s):
        grid = both_ways(grid, dft4)
        for k in range(4):
            for l in range(4):
                store(x_ref, k, l, s, grid[k][l])

    def gathered_up(s):
        return both_ways([[load(y_ref, k, l, s) for l in range(4)] for k in range(4)], idft4)

    def operate(strip, meanwhile=None):
        for k in range(4):
            cols = []
            for l in range(4):
                parts = [
                    x_ref[c, k, :, l * W + u * B : l * W + (u + 1) * B] for c in range(2) for u in range(2)
                ]
                cols.append(jnp.concatenate(parts, axis=0))
            z = dot(left[k], jnp.concatenate(cols, axis=1))
            for l in range(4):
                v = jnp.concatenate([z[:B, lanes(l)], z[B:, lanes(l)]], axis=1)
                v_ref[l, k * B : (k + 1) * B, :] = v.astype(BF16)
            if meanwhile is not None:
                meanwhile(2 * k)
                meanwhile(2 * k + 1)
        for chunk in range(CHUNKS):
            size = U // CHUNKS
            rows = slice(chunk * size, (chunk + 1) * size)
            for l in range(4):
                parts = [
                    v_ref[l, k * B + u * U + chunk * size : k * B + u * U + (chunk + 1) * size, :]
                    for k in range(4)
                    for u in range(2)
                ]
                y = dot(jnp.concatenate(parts, axis=0), right[l])
                for k in range(4):
                    for c in range(2):
                        at = y[2 * k * size : (2 * k + 2) * size, lanes(c)]
                        both = jnp.concatenate([at[:size], at[size:]], axis=1)
                        y_ref[c, k, rows, wide(l)] = both.astype(BF16)
            if chunk:
                for s in range(STRIPS // CHUNKS):
                    strip((chunk - 1) * (STRIPS // CHUNKS) + s)
        for s in range(STRIPS // CHUNKS):
            strip((CHUNKS - 1) * (STRIPS // CHUNKS) + s)

    def masked(plane, field, k, l, s):
        g = mul(field, load(mask_ref.at[plane], k, l, s))
        store(g_ref.at[plane], k, l, s, g)
        return g

    def first_strip(s):
        decode(0, s)

        def at(k, l):
            field = (source_x[k, rows_of(s), :] * source_y[l, 0:1]).astype(BF16)
            mask = load(mask_ref.at[0], k, l, s)
            g = (field * mask[0], field * mask[1])
            store(g_ref.at[0], k, l, s, g)
            return g

        spread_out([[at(k, l) for l in range(4)] for k in range(4)], s)

    def forward_strip(plane, s):
        field = gathered_up(s)
        spread_out([[masked(plane, field[k][l], k, l, s) for l in range(4)] for k in range(4)], s)

    def last_strip(s):
        field = gathered_up(s)
        for k in range(4):
            a = (far_x[0, k, rows_of(s), :], far_x[1, k, rows_of(s), :])
            for l in range(4):
                part = mul(masked(PLANES - 1, field[k][l], k, l, s), a)
                sums[l] = add(sums[l], (part[0].astype(F32), part[1].astype(F32)))

    def returned(plane, back, k, l, s):
        g = load(g_ref.at[plane], k, l, s)
        half, group, rows = piece_of(k, s)
        grad[half, (k % 2) * GROUPS + group + l // 2, plane, l % 2, rows] = back[0] * g[1] + back[1] * g[0]
        return mul(back, load(mask_ref.at[plane], k, l, s)) if plane else None

    for copy in arrivals:
        copy.wait()
    for s in range(STRIPS):
        first_strip(s)
    for plane in range(1, PLANES - 1):
        operate(functools.partial(forward_strip, plane), functools.partial(decode, plane))
    nothing = jnp.zeros((STRIP, W), F32)
    sums = [(nothing, nothing) for _ in range(4)]
    operate(last_strip, functools.partial(decode, PLANES - 1))
    far = [(far_y[0, l], far_y[1, l]) for l in range(4)]
    total = [mul(s, y) for s, y in zip(sums, far)]
    coupling_re = jnp.sum(sum(t[0] for t in total))
    coupling_im = jnp.sum(sum(t[1] for t in total))
    back_y = [
        (
            (coupling_re * y[0] + coupling_im * y[1]).astype(BF16),
            (coupling_re * y[1] - coupling_im * y[0]).astype(BF16),
        )
        for y in far
    ]

    def turn_strip(s):
        def at(k, l):
            a = (far_x[0, k, rows_of(s), :], far_x[1, k, rows_of(s), :])
            return returned(PLANES - 1, mul(a, back_y[l]), k, l, s)

        spread_out([[at(k, l) for l in range(4)] for k in range(4)], s)

    def backward_strip(plane, s):
        back = gathered_up(s)
        reply = [[returned(plane, back[k][l], k, l, s) for l in range(4)] for k in range(4)]
        if plane:
            spread_out(reply, s)

    for s in range(STRIPS):
        turn_strip(s)
    for plane in reversed(range(PLANES - 1)):
        operate(functools.partial(backward_strip, plane))
    departures = [
        pltpu.make_async_copy(grad.at[1 - core], send, sems.at[0]),
        pltpu.make_async_copy(grad.at[core], keep, sems.at[1]),
    ]
    for copy in departures:
        copy.start()
    for copy in departures:
        copy.wait()


def main_call(plane_id, core_id, side_id, tan_own, tan_in, tables):
    half = (2 * GROUPS, PLANES, 2, *PIECE)
    return pl.pallas_call(
        main_kernel,
        name="modes",
        in_specs=[SMEM] * 3 + [ANY] * 7 + [VMEM] * 6,
        out_specs=[ANY, ANY],
        out_shape=[jax.ShapeDtypeStruct(half, BF16)] * 2,
        scratch_shapes=[
            pltpu.VMEM((2, 4, U, WIDE), BF16),
            pltpu.VMEM((4, N, 2 * B), BF16),
            pltpu.VMEM((2, 4, U, WIDE), BF16),
            pltpu.VMEM((PLANES, 2, 4, U, WIDE), BF16),
            pltpu.VMEM((PLANES, 2, 4, U, WIDE), BF16),
            pltpu.VMEM((PLANES, 2, 2, GROUPS, 2, *PIECE), BF16),
            pltpu.VMEM((2, *half), BF16),
            pltpu.SemaphoreType.DMA((7,)),
        ],
        compiler_params=vmem_limit(26),
    )(plane_id, core_id, side_id, tan_own, *tan_in, *tables)


def tangents_of_row(phase, first, out):
    def strip(r, carry):
        for u in range(2):
            rows = pl.ds(pl.multiple_of(first + u * U + r * PIECE[0], PIECE[0]), PIECE[0])
            for l in range(4):
                out[2 * r + l // 2, l % 2, :, lanes(u)] = half_angle_tangent(phase[rows, lanes(l)]).astype(BF16)
        return carry

    lax.fori_loop(0, U // PIECE[0], strip, 0)


def tangent_kernel(row_id, phase, out, rows, sem):
    copy = pltpu.make_async_copy(phase.at[0, pl.ds(row_id[0] * B, B)], rows, sem)
    copy.start()
    copy.wait()
    tangents_of_row(rows, 0, out)


def tangent_call(row_id, phase_masks):
    return pl.pallas_call(
        tangent_kernel,
        name="tangent",
        in_specs=[SMEM, HBM],
        out_specs=VMEM,
        out_shape=jax.ShapeDtypeStruct((GROUPS, 2, *PIECE), BF16),
        scratch_shapes=[pltpu.VMEM((B, N), F32), pltpu.SemaphoreType.DMA],
        compiler_params=vmem_limit(59),
    )(row_id, phase_masks)


def own_tangent_kernel(phase, out):
    for k in range(4):
        tangents_of_row(phase.at[0], k * B, out.at[k // 2, k % 2])


def own_tangent_call(phase_masks):
    return pl.pallas_call(
        own_tangent_kernel,
        name="own_tangent",
        in_specs=[VMEM],
        out_specs=VMEM,
        out_shape=jax.ShapeDtypeStruct((2, 2, GROUPS, 2, *PIECE), BF16),
        compiler_params=vmem_limit(6),
    )(phase_masks)


def rows_of_group(half, group, u):
    k, r = 2 * half + group // GROUPS, (group % GROUPS) // 2
    return pl.ds(k * B + u * U + r * PIECE[0], PIECE[0])


def cols_of_group(group, n):
    return lanes(2 * (group % 2) + n)


def finish_kernel(core_id, phase_in, own, other, out, phase, sem):
    arrival = pltpu.make_async_copy(phase_in, phase, sem)
    arrival.start()
    squares = jnp.zeros(PIECE, F32)
    for group in range(2 * GROUPS):
        for n in range(2):
            for part in (own, other):
                x = part[group, n].astype(F32)
                squares += x * x
    mean = 4.0 * jnp.sum(squares, keepdims=True) / (N * N)
    scale = -2.0 * lax.rsqrt(mean + EPSILON)
    core = core_id[0]
    arrival.wait()
    for part, half in ((own, core), (other, 1 - core)):
        for group in range(2 * GROUPS):
            for n in range(2):
                for u in range(2):
                    rows, cols = rows_of_group(half, group, u), cols_of_group(group, n)
                    step = part[group, n, :, lanes(u)].astype(F32) * scale
                    out[0, rows, cols] = phase[0, rows, cols] + step


def finish_call(core_id, phase_masks, own, other):
    return pl.pallas_call(
        finish_kernel,
        name="finish",
        in_specs=[SMEM, HBM, VMEM, VMEM],
        out_specs=VMEM,
        out_shape=jax.ShapeDtypeStruct((1, N, N), F32),
        scratch_shapes=[pltpu.VMEM((1, N, N), F32), pltpu.SemaphoreType.DMA],
        compiler_params=vmem_limit(8),
    )(core_id, phase_masks, own, other)


def swapped(x):
    return lax.ppermute(x, CORE, [(0, 1), (1, 0)])


def shifted(x, step):
    return lax.ppermute(x, "mode_0", [(i, (i + step) % 4) for i in range(4)])


def from_plane(x, step):
    across = 1 if step == 2 else 0
    here = [(p, z) for p in range(PLANES) for z in range(2)]
    there = [((p + step) % PLANES * 2 + (z ^ across), 2 * p + z) for p, z in here]
    return lax.ppermute(x, Z, there)


def exchanged(x, axes):
    return lax.all_to_all(x, axes, split_axis=0, concat_axis=0, tiled=True)


def from_everyone(x, axes):
    count = lax.axis_size(axes)
    return exchanged(jnp.broadcast_to(x[None], (count, *x.shape)), axes)


def shards(phase_masks, hg_orders, spot_index):
    core_id = lax.axis_index(CORE).astype(jnp.int32)[None]
    plane_id = lax.axis_index("plane").astype(jnp.int32)[None]
    side_id = (lax.axis_index("mode_0").astype(jnp.int32) & 1)[None]
    tangent = tangent_call(2 * core_id + side_id, phase_masks)
    arriving = [from_plane(tangent, step) for step in (1, 2, -1)]
    tan_own = own_tangent_call(phase_masks)
    tables = setup_call(plane_id, hg_orders.T, spot_index, *block_operators())
    arrived, tan_own, tables = lax.optimization_barrier((arriving, tan_own, tables))
    straight = jnp.stack(arrived)
    before = shifted(straight[:, : GROUPS // 2], 1)
    after = shifted(straight[:, GROUPS // 2 :], -1)
    half_own = [straight, before, after]
    tan_in = half_own + [swapped(x) for x in half_own]
    keep, send = main_call(plane_id, core_id, side_id, tan_own, tan_in, tables)
    pair = keep + swapped(send)
    column = jnp.sum(exchanged(pair, XY).astype(F32), axis=0).astype(BF16)
    pieces = jnp.repeat(column, 2, axis=0)
    total = jnp.sum(exchanged(pieces, Z).astype(F32), axis=0).astype(BF16)
    own = from_everyone(total, XY)
    other = swapped(own)
    return finish_call(core_id, phase_masks, own, other)


def solution(mesh):
    finer = Mesh(
        mesh.devices.reshape(mesh.shape["plane"], 4, 4, 2, 2),
        ("plane", "mode_0", "mode_1", "mode_2", "mode_3"),
    )
    placed = (P("plane", None, None), P(MODE, None), P(MODE))
    return jax.shard_map(
        shards, mesh=finer, in_specs=placed, out_specs=P("plane", None, None), check_vma=False
    )
```

```python
import functools
import math

import jax
import jax.numpy as jnp
import numpy as np
from jax import lax
from jax.experimental import pallas as pl
from jax.experimental.pallas import tpu as pltpu
from jax.sharding import Mesh
from jax.sharding import PartitionSpec as P

ORDERS = 45
SPOT_SIDE = 32
MODE = ("mode_0", "mode_1", "mode_2", "mode_3")
XY = ("mode_0", "mode_1")
Z = ("plane", "mode_2")
CORE = "mode_3"
PLANES = 4
N = 512
B = 128
U = B // 2
W = 2 * B
WIDE = 4 * W
STRIP = 8
STRIPS = U // STRIP
CHUNKS = 4
PIECE = (16, W)
GROUPS = 8
CHIRP_RATE = math.pi / 48.0 * (math.pi / 48.0)
AMPLITUDE = 12.0
EPSILON = 1e-06
F32 = jnp.float32
BF16 = jnp.bfloat16
SMEM = pl.BlockSpec(memory_space=pltpu.SMEM)
VMEM = pl.BlockSpec(memory_space=pltpu.VMEM)
ANY = pl.BlockSpec(memory_space=pl.ANY)
HBM = pl.BlockSpec(memory_space=pltpu.HBM)


def vmem_limit(mib):
    return pltpu.CompilerParams(vmem_limit_bytes=mib << 20)


def block_operators():
    f = np.arange(N)
    s = (f + N // 2) % N - N // 2
    chirp = np.exp(-1j * CHIRP_RATE * s.astype(np.float64) ** 2)
    phase = np.exp(2j * np.pi * ((f[:, None] * f[None, :]) % N) / N)
    kernel = (phase * chirp[None, :]).sum(axis=1) / N
    offset = np.arange(B)[:, None] - np.arange(B)[None, :]
    left, right = [], []
    for k in range(4):
        block = sum((-1j) ** (k * m) * kernel[(offset + B * m) % N] for m in range(4)) / 4.0
        real = np.block([[block.real, -block.imag], [block.imag, block.real]])
        left.append(real)
        right.append(real.T)
    to = lambda x: jnp.asarray(np.stack(x).astype(np.float32)).astype(BF16)
    return to(left), to(right)


def add(x, y):
    return (x[0] + y[0], x[1] + y[1])


def sub(x, y):
    return (x[0] - y[0], x[1] - y[1])


def turned(x, y):
    return (x[0] - y[1], x[1] + y[0])


def turned_back(x, y):
    return (x[0] + y[1], x[1] - y[0])


def dft4(x):
    a, b, c, d = add(x[0], x[2]), sub(x[0], x[2]), add(x[1], x[3]), sub(x[1], x[3])
    return [add(a, c), turned_back(b, d), sub(a, c), turned(b, d)]


def idft4(x):
    a, b, c, d = add(x[0], x[2]), sub(x[0], x[2]), add(x[1], x[3]), sub(x[1], x[3])
    return [add(a, c), turned(b, d), sub(a, c), turned_back(b, d)]


def both_ways(grid, transform):
    grid = [transform(row) for row in grid]
    cols = [transform([grid[k][l] for k in range(4)]) for l in range(4)]
    return [[cols[l][k] for l in range(4)] for k in range(4)]


def mul(x, y):
    return (x[0] * y[0] - x[1] * y[1], x[0] * y[1] + x[1] * y[0])


def dot(a, b):
    return jnp.dot(a, b, preferred_element_type=F32)


def lanes(l):
    return slice(l * B, (l + 1) * B)


def half_angle_tangent(phase):
    x = 0.5 * phase
    y = x * x
    sine, cosine = 0.0, 0.0
    for n in reversed(range(7)):
        sine = sine * y + (-1) ** n / math.factorial(2 * n + 1)
        cosine = cosine * y + (-1) ** n / math.factorial(2 * n)
    return x * sine / cosine


def hermite_tables(psi):
    t = (lax.broadcasted_iota(jnp.int32, (8, N), 1).astype(F32) - (N - 1) / 2.0) / (N / 48.0)
    previous = math.pow(math.pi, -0.25) * jnp.exp(-0.5 * t * t)
    current = math.sqrt(2.0) * t * previous
    psi[0] = previous
    psi[1] = current
    for n in range(1, ORDERS - 1):
        higher = math.sqrt(2.0 / (n + 1.0)) * t * current - math.sqrt(n / (n + 1.0)) * previous
        psi[n + 1] = higher
        previous, current = current, higher


def spot_profile(index, shape, dim):
    coords = lax.broadcasted_iota(jnp.int32, shape, dim).astype(F32) - (N - 1) / 2.0
    centre = index.astype(F32) - (SPOT_SIDE - 1) / 2.0
    offset = (coords - (N / 40.0) * centre) / (N / 120.0)
    return jnp.exp(-offset * offset)


def split(x):
    high = x.astype(BF16)
    return high, (x - high.astype(F32)).astype(BF16)


def wide(l):
    return slice(l * W, (l + 1) * W)


def beside(x):
    return jnp.concatenate([x[:U], x[U:]], axis=1)


def setup_kernel(plane_id, orders_in, spots_in, left_in, right_in, left, right, source_x, source_y, far_x, far_y,
                 orders, spots, psi, sems):
    mode = plane_id[0]
    pairs = [(orders_in, orders), (spots_in, spots), (left_in, left), (right_in, right)]
    arrivals = [pltpu.make_async_copy(*pair, sems.at[n]) for n, pair in enumerate(pairs)]
    for copy in arrivals:
        copy.start()
    for copy in arrivals[:2]:
        copy.wait()
    hermite_tables(psi)
    row = psi[orders[1, mode]]
    for l in range(4):
        source_y[l] = jnp.concatenate([row[:, lanes(l)]] * 2, axis=1)
    row = AMPLITUDE * psi[orders[0, mode]][0:1]
    for k in range(4):
        source_x[k] = beside(jnp.broadcast_to(row[:, lanes(k)], (B, B)).T)

    for copy in arrivals[2:]:
        copy.wait()
    spot = spots[mode]
    down = spot_profile(spot // SPOT_SIDE, (N, B), 0)
    zero = jnp.zeros((B, B), F32)
    spread = dft4([(down[k * B : (k + 1) * B], zero) for k in range(4)])
    moved = []
    for k in range(4):
        high, low = split(jnp.concatenate(spread[k], axis=0))
        both = dot(left[k], jnp.concatenate([high, low], axis=1))
        total = both[:, :B] + both[:, B:]
        moved.append((total[:B], total[B:]))
    for k, part in enumerate(idft4(moved)):
        far_x[0, k] = beside(part[0]).astype(BF16)
        far_x[1, k] = beside(part[1]).astype(BF16)
    along = spot_profile(spot % SPOT_SIDE, (8, N), 1)
    zero = jnp.zeros((8, B), F32)
    spread = dft4([(along[:, lanes(l)], zero) for l in range(4)])
    moved = []
    for l in range(4):
        high, low = split(jnp.concatenate(spread[l], axis=1))
        both = dot(jnp.concatenate([high, low], axis=0), right[l])
        total = both[:8] + both[8:]
        moved.append((total[:, :B], total[:, B:]))
    for l, y in enumerate(idft4(moved)):
        for c in range(2):
            far_y[c, l] = jnp.concatenate([y[c]] * 2, axis=1)


def setup_call(plane_id, orders, spots, left, right):
    return pl.pallas_call(
        setup_kernel,
        name="setup",
        in_specs=[SMEM, HBM, HBM, HBM, HBM],
        out_specs=[VMEM] * 6,
        out_shape=[
            jax.ShapeDtypeStruct(left.shape, BF16),
            jax.ShapeDtypeStruct(right.shape, BF16),
            jax.ShapeDtypeStruct((4, U, W), F32),
            jax.ShapeDtypeStruct((4, 8, W), F32),
            jax.ShapeDtypeStruct((2, 4, U, W), BF16),
            jax.ShapeDtypeStruct((2, 4, 8, W), F32),
        ],
        scratch_shapes=[
            pltpu.SMEM((2, PLANES), jnp.int32),
            pltpu.SMEM((PLANES,), jnp.int32),
            pltpu.VMEM((ORDERS, 8, N), F32),
            pltpu.SemaphoreType.DMA((4,)),
        ],
        compiler_params=vmem_limit(8),
    )(plane_id, orders, spots, left, right)


def main_kernel(
    plane_id, core_id, side_id, tan_own, *refs,
):
    tan_in, (left, right, source_x, source_y, far_x, far_y, keep, send) = refs[:6], refs[6:14]
    x_ref, v_ref, y_ref, g_ref, mask_ref, tan_ref, grad, sems = refs[14:]
    mode, core, side = plane_id[0], core_id[0], side_id[0]
    pairs = [(tan_own, tan_ref.at[0])]
    for at, (straight, before, after) in ((core, tan_in[:3]), (1 - core, tan_in[3:])):
        across = slice(1, PLANES)
        pairs.append((straight, tan_ref.at[across, at, side]))
        pairs.append((before, tan_ref.at[across, at, 1 - side, 0 : GROUPS // 2]))
        pairs.append((after, tan_ref.at[across, at, 1 - side, GROUPS // 2 : GROUPS]))
    arrivals = [pltpu.make_async_copy(*pair, sems.at[n]) for n, pair in enumerate(pairs)]
    for copy in arrivals:
        copy.start()

    def rows_of(s):
        return slice(s * STRIP, (s + 1) * STRIP)

    def piece_of(k, s):
        return k // 2, (s // 2) * 2, slice((s % 2) * STRIP, (s % 2 + 1) * STRIP)

    def decode(plane, s):
        for k in range(4):
            half, group, rows = piece_of(k, s)
            for l in range(4):
                t = tan_ref[(plane - mode) & 3, half, k % 2, group + l // 2, l % 2, rows].astype(F32)
                twice = 2.0 / (1.0 + t * t)
                mask_ref[plane, 0, k, rows_of(s), wide(l)] = (twice - 1.0).astype(BF16)
                mask_ref[plane, 1, k, rows_of(s), wide(l)] = (twice * t).astype(BF16)

    def load(ref, k, l, s):
        return (ref[0, k, rows_of(s), wide(l)], ref[1, k, rows_of(s), wide(l)])

    def store(ref, k, l, s, x):
        ref[0, k, rows_of(s), wide(l)] = x[0]
        ref[1, k, rows_of(s), wide(l)] = x[1]

    def spread_out(grid, s):
        grid = both_ways(grid, dft4)
        for k in range(4):
            for l in range(4):
                store(x_ref, k, l, s, grid[k][l])

    def gathered_up(s):
        return both_ways([[load(y_ref, k, l, s) for l in range(4)] for k in range(4)], idft4)

    def operate(strip, meanwhile=None):
        for k in range(4):
            cols = []
            for l in range(4):
                parts = [
                    x_ref[c, k, :, l * W + u * B : l * W + (u + 1) * B] for c in range(2) for u in range(2)
                ]
                cols.append(jnp.concatenate(parts, axis=0))
            z = dot(left[k], jnp.concatenate(cols, axis=1))
            for l in range(4):
                v = jnp.concatenate([z[:B, lanes(l)], z[B:, lanes(l)]], axis=1)
                v_ref[l, k * B : (k + 1) * B, :] = v.astype(BF16)
            if meanwhile is not None:
                meanwhile(2 * k)
                meanwhile(2 * k + 1)
        for chunk in range(CHUNKS):
            size = U // CHUNKS
            rows = slice(chunk * size, (chunk + 1) * size)
            for l in range(4):
                parts = [
                    v_ref[l, k * B + u * U + chunk * size : k * B + u * U + (chunk + 1) * size, :]
                    for k in range(4)
                    for u in range(2)
                ]
                y = dot(jnp.concatenate(parts, axis=0), right[l])
                for k in range(4):
                    for c in range(2):
                        at = y[2 * k * size : (2 * k + 2) * size, lanes(c)]
                        both = jnp.concatenate([at[:size], at[size:]], axis=1)
                        y_ref[c, k, rows, wide(l)] = both.astype(BF16)
            if chunk:
                for s in range(STRIPS // CHUNKS):
                    strip((chunk - 1) * (STRIPS // CHUNKS) + s)
        for s in range(STRIPS // CHUNKS):
            strip((CHUNKS - 1) * (STRIPS // CHUNKS) + s)

    def masked(plane, field, k, l, s):
        g = mul(field, load(mask_ref.at[plane], k, l, s))
        store(g_ref.at[plane], k, l, s, g)
        return g

    def first_strip(s):
        decode(0, s)

        def at(k, l):
            field = (source_x[k, rows_of(s), :] * source_y[l, 0:1]).astype(BF16)
            mask = load(mask_ref.at[0], k, l, s)
            g = (field * mask[0], field * mask[1])
            store(g_ref.at[0], k, l, s, g)
            return g

        spread_out([[at(k, l) for l in range(4)] for k in range(4)], s)

    def forward_strip(plane, s):
        field = gathered_up(s)
        spread_out([[masked(plane, field[k][l], k, l, s) for l in range(4)] for k in range(4)], s)

    def last_strip(s):
        field = gathered_up(s)
        for k in range(4):
            a = (far_x[0, k, rows_of(s), :], far_x[1, k, rows_of(s), :])
            for l in range(4):
                part = mul(masked(PLANES - 1, field[k][l], k, l, s), a)
                sums[l] = add(sums[l], (part[0].astype(F32), part[1].astype(F32)))

    def returned(plane, back, k, l, s):
        g = load(g_ref.at[plane], k, l, s)
        half, group, rows = piece_of(k, s)
        grad[half, (k % 2) * GROUPS + group + l // 2, plane, l % 2, rows] = back[0] * g[1] + back[1] * g[0]
        return mul(back, load(mask_ref.at[plane], k, l, s)) if plane else None

    for copy in arrivals:
        copy.wait()
    for s in range(STRIPS):
        first_strip(s)
    for plane in range(1, PLANES - 1):
        operate(functools.partial(forward_strip, plane), functools.partial(decode, plane))
    nothing = jnp.zeros((STRIP, W), F32)
    sums = [(nothing, nothing) for _ in range(4)]
    operate(last_strip, functools.partial(decode, PLANES - 1))
    far = [(far_y[0, l], far_y[1, l]) for l in range(4)]
    total = [mul(s, y) for s, y in zip(sums, far)]
    coupling_re = jnp.sum(sum(t[0] for t in total))
    coupling_im = jnp.sum(sum(t[1] for t in total))
    back_y = [
        (
            (coupling_re * y[0] + coupling_im * y[1]).astype(BF16),
            (coupling_re * y[1] - coupling_im * y[0]).astype(BF16),
        )
        for y in far
    ]

    def turn_strip(s):
        def at(k, l):
            a = (far_x[0, k, rows_of(s), :], far_x[1, k, rows_of(s), :])
            return returned(PLANES - 1, mul(a, back_y[l]), k, l, s)

        spread_out([[at(k, l) for l in range(4)] for k in range(4)], s)

    def backward_strip(plane, s):
        back = gathered_up(s)
        reply = [[returned(plane, back[k][l], k, l, s) for l in range(4)] for k in range(4)]
        if plane:
            spread_out(reply, s)

    for s in range(STRIPS):
        turn_strip(s)
    for plane in reversed(range(PLANES - 1)):
        operate(functools.partial(backward_strip, plane))
    departures = [
        pltpu.make_async_copy(grad.at[1 - core], send, sems.at[0]),
        pltpu.make_async_copy(grad.at[core], keep, sems.at[1]),
    ]
    for copy in departures:
        copy.start()
    for copy in departures:
        copy.wait()


def main_call(plane_id, core_id, side_id, tan_own, tan_in, tables):
    half = (2 * GROUPS, PLANES, 2, *PIECE)
    return pl.pallas_call(
        main_kernel,
        name="modes",
        in_specs=[SMEM] * 3 + [ANY] * 7 + [VMEM] * 6,
        out_specs=[ANY, ANY],
        out_shape=[jax.ShapeDtypeStruct(half, BF16)] * 2,
        scratch_shapes=[
            pltpu.VMEM((2, 4, U, WIDE), BF16),
            pltpu.VMEM((4, N, 2 * B), BF16),
            pltpu.VMEM((2, 4, U, WIDE), BF16),
            pltpu.VMEM((PLANES, 2, 4, U, WIDE), BF16),
            pltpu.VMEM((PLANES, 2, 4, U, WIDE), BF16),
            pltpu.VMEM((PLANES, 2, 2, GROUPS, 2, *PIECE), BF16),
            pltpu.VMEM((2, *half), BF16),
            pltpu.SemaphoreType.DMA((7,)),
        ],
        compiler_params=vmem_limit(26),
    )(plane_id, core_id, side_id, tan_own, *tan_in, *tables)


def tangents_of_strip(phase, first, r, out):
    for u in range(2):
        rows = slice(first + u * U + r * PIECE[0], first + u * U + (r + 1) * PIECE[0])
        for l in range(4):
            out[2 * r + l // 2, l % 2, :, lanes(u)] = half_angle_tangent(phase[rows, lanes(l)]).astype(BF16)


def tangent_kernel(row_id, phase, out, rows, tangents, sems_in, sems_out):
    strips = U // PIECE[0]
    arrivals, departures = [], []
    for r in range(strips):
        for u in range(2):
            at = pl.ds(row_id[0] * B + u * U + r * PIECE[0], PIECE[0])
            here = rows.at[u * U + r * PIECE[0] : u * U + (r + 1) * PIECE[0]]
            arrivals.append(pltpu.make_async_copy(phase.at[0, at], here, sems_in.at[2 * r + u]))
        pair = slice(2 * r, 2 * r + 2)
        departures.append(pltpu.make_async_copy(tangents.at[pair], out.at[pair], sems_out.at[r]))
    for copy in arrivals:
        copy.start()
    for r in range(strips):
        arrivals[2 * r].wait()
        arrivals[2 * r + 1].wait()
        tangents_of_strip(rows, 0, r, tangents)
        departures[r].start()
    for copy in departures:
        copy.wait()


def tangent_call(row_id, phase_masks):
    return pl.pallas_call(
        tangent_kernel,
        name="tangent",
        in_specs=[SMEM, HBM],
        out_specs=HBM,
        out_shape=jax.ShapeDtypeStruct((GROUPS, 2, *PIECE), BF16),
        scratch_shapes=[
            pltpu.VMEM((B, N), F32),
            pltpu.VMEM((GROUPS, 2, *PIECE), BF16),
            pltpu.SemaphoreType.DMA((2 * U // PIECE[0],)),
            pltpu.SemaphoreType.DMA((U // PIECE[0],)),
        ],
        compiler_params=vmem_limit(59),
    )(row_id, phase_masks)


def own_tangent_kernel(phase, out):
    def row(k, carry):
        for r in range(U // PIECE[0]):
            tangents_of_strip(phase.at[0, pl.ds(pl.multiple_of(k * B, B), B)], 0, r, out.at[k // 2, k % 2])
        return carry

    lax.fori_loop(0, 4, row, 0)


def own_tangent_call(phase_masks):
    return pl.pallas_call(
        own_tangent_kernel,
        name="own_tangent",
        in_specs=[VMEM],
        out_specs=VMEM,
        out_shape=jax.ShapeDtypeStruct((2, 2, GROUPS, 2, *PIECE), BF16),
        compiler_params=vmem_limit(6),
    )(phase_masks)


def rows_of_group(half, group, u):
    k, r = 2 * half + group // GROUPS, (group % GROUPS) // 2
    return pl.ds(k * B + u * U + r * PIECE[0], PIECE[0])


def cols_of_group(group, n):
    return lanes(2 * (group % 2) + n)


def finish_kernel(core_id, phase, own, other, out, result, sems):
    squares = jnp.zeros(PIECE, F32)
    for group in range(2 * GROUPS):
        for n in range(2):
            for part in (own, other):
                x = part[group, n].astype(F32)
                squares += x * x
    mean = 4.0 * jnp.sum(squares, keepdims=True) / (N * N)
    scale = -2.0 * lax.rsqrt(mean + EPSILON)
    core = core_id[0]
    departures = []
    for part, half in ((own, core), (other, 1 - core)):
        for side in range(2):
            for group in range(side * GROUPS, (side + 1) * GROUPS):
                for n in range(2):
                    for u in range(2):
                        rows, cols = rows_of_group(half, group, u), cols_of_group(group, n)
                        step = part[group, n, :, lanes(u)].astype(F32) * scale
                        result[rows, cols] = phase[0, rows, cols] + step
            done = pl.ds(pl.multiple_of((2 * half + side) * B, B), B)
            copy = pltpu.make_async_copy(result.at[done], out.at[0, done], sems.at[len(departures)])
            copy.start()
            departures.append(copy)
    for copy in departures:
        copy.wait()


def finish_call(core_id, phase_masks, own, other):
    return pl.pallas_call(
        finish_kernel,
        name="finish",
        in_specs=[SMEM, VMEM, VMEM, VMEM],
        out_specs=HBM,
        out_shape=jax.ShapeDtypeStruct((1, N, N), F32),
        scratch_shapes=[pltpu.VMEM((N, N), F32), pltpu.SemaphoreType.DMA((4,))],
        compiler_params=vmem_limit(8),
    )(core_id, phase_masks, own, other)


def swapped(x):
    return lax.ppermute(x, CORE, [(0, 1), (1, 0)])


def shifted(x, step):
    return lax.ppermute(x, "mode_0", [(i, (i + step) % 4) for i in range(4)])


def from_plane(x, step):
    across = 1 if step == 2 else 0
    here = [(p, z) for p in range(PLANES) for z in range(2)]
    there = [((p + step) % PLANES * 2 + (z ^ across), 2 * p + z) for p, z in here]
    return lax.ppermute(x, Z, there)


def exchanged(x, axes):
    return lax.all_to_all(x, axes, split_axis=0, concat_axis=0, tiled=True)


def from_everyone(x, axes):
    count = lax.axis_size(axes)
    return exchanged(jnp.broadcast_to(x[None], (count, *x.shape)), axes)


def shards(phase_masks, hg_orders, spot_index):
    core_id = lax.axis_index(CORE).astype(jnp.int32)[None]
    plane_id = lax.axis_index("plane").astype(jnp.int32)[None]
    side_id = (lax.axis_index("mode_0").astype(jnp.int32) & 1)[None]
    tangent = tangent_call(2 * core_id + side_id, phase_masks)
    arriving = [from_plane(tangent, step) for step in (1, 2, -1)]
    tan_own = own_tangent_call(phase_masks)
    tables = setup_call(plane_id, hg_orders.T, spot_index, *block_operators())
    arrived, tan_own, tables = lax.optimization_barrier((arriving, tan_own, tables))
    straight = jnp.stack(arrived)
    before = shifted(straight[:, : GROUPS // 2], 1)
    after = shifted(straight[:, GROUPS // 2 :], -1)
    half_own = [straight, before, after]
    tan_in = half_own + [swapped(x) for x in half_own]
    keep, send = main_call(plane_id, core_id, side_id, tan_own, tan_in, tables)
    pair = keep + swapped(send)
    column = jnp.sum(exchanged(pair, XY).astype(F32), axis=0).astype(BF16)
    pieces = jnp.repeat(column, 2, axis=0)
    total = jnp.sum(exchanged(pieces, Z).astype(F32), axis=0).astype(BF16)
    own = from_everyone(total, XY)
    other = swapped(own)
    return finish_call(core_id, phase_masks, own, other)


def solution(mesh):
    finer = Mesh(
        mesh.devices.reshape(mesh.shape["plane"], 4, 4, 2, 2),
        ("plane", "mode_0", "mode_1", "mode_2", "mode_3"),
    )
    placed = (P("plane", None, None), P(MODE, None), P(MODE))
    return jax.shard_map(
        shards, mesh=finer, in_specs=placed, out_specs=P("plane", None, None), check_vma=False
    )
```

```python
import functools
import math

import jax
import jax.numpy as jnp
import numpy as np
from jax import lax
from jax.experimental import pallas as pl
from jax.experimental.pallas import tpu as pltpu
from jax.sharding import Mesh
from jax.sharding import PartitionSpec as P

ORDERS = 45
SPOT_SIDE = 32
MODE = ("mode_0", "mode_1", "mode_2", "mode_3")
XY = ("mode_0", "mode_1")
CHIPS = ("mode_0", "mode_1", "mode_2")
Z = ("plane", "mode_2")
CORE = "mode_3"
PLANES = 4
N = 512
B = 128
U = B // 2
W = 2 * B
WIDE = 4 * W
STRIP = 8
STRIPS = U // STRIP
CHUNKS = 4
PIECE = (16, W)
GROUPS = 8
CHIRP_RATE = math.pi / 48.0 * (math.pi / 48.0)
AMPLITUDE = 12.0
EPSILON = 1e-06
F32 = jnp.float32
BF16 = jnp.bfloat16
SMEM = pl.BlockSpec(memory_space=pltpu.SMEM)
VMEM = pl.BlockSpec(memory_space=pltpu.VMEM)
ANY = pl.BlockSpec(memory_space=pl.ANY)
HBM = pl.BlockSpec(memory_space=pltpu.HBM)


def vmem_limit(mib):
    return pltpu.CompilerParams(vmem_limit_bytes=mib << 20)


def block_operators():
    f = np.arange(N)
    s = (f + N // 2) % N - N // 2
    chirp = np.exp(-1j * CHIRP_RATE * s.astype(np.float64) ** 2)
    phase = np.exp(2j * np.pi * ((f[:, None] * f[None, :]) % N) / N)
    kernel = (phase * chirp[None, :]).sum(axis=1) / N
    offset = np.arange(B)[:, None] - np.arange(B)[None, :]
    left, right = [], []
    for k in range(4):
        block = sum((-1j) ** (k * m) * kernel[(offset + B * m) % N] for m in range(4)) / 4.0
        real = np.block([[block.real, -block.imag], [block.imag, block.real]])
        left.append(real)
        right.append(real.T)
    to = lambda x: jnp.asarray(np.stack(x).astype(np.float32)).astype(BF16)
    return to(left), to(right)


def add(x, y):
    return (x[0] + y[0], x[1] + y[1])


def sub(x, y):
    return (x[0] - y[0], x[1] - y[1])


def turned(x, y):
    return (x[0] - y[1], x[1] + y[0])


def turned_back(x, y):
    return (x[0] + y[1], x[1] - y[0])


def dft4(x):
    a, b, c, d = add(x[0], x[2]), sub(x[0], x[2]), add(x[1], x[3]), sub(x[1], x[3])
    return [add(a, c), turned_back(b, d), sub(a, c), turned(b, d)]


def idft4(x):
    a, b, c, d = add(x[0], x[2]), sub(x[0], x[2]), add(x[1], x[3]), sub(x[1], x[3])
    return [add(a, c), turned(b, d), sub(a, c), turned_back(b, d)]


def both_ways(grid, transform):
    grid = [transform(row) for row in grid]
    cols = [transform([grid[k][l] for k in range(4)]) for l in range(4)]
    return [[cols[l][k] for l in range(4)] for k in range(4)]


def mul(x, y):
    return (x[0] * y[0] - x[1] * y[1], x[0] * y[1] + x[1] * y[0])


def dot(a, b):
    return jnp.dot(a, b, preferred_element_type=F32)


def lanes(l):
    return slice(l * B, (l + 1) * B)


def half_angle_tangent(phase):
    x = 0.5 * phase
    y = x * x
    sine, cosine = 0.0, 0.0
    for n in reversed(range(7)):
        sine = sine * y + (-1) ** n / math.factorial(2 * n + 1)
        cosine = cosine * y + (-1) ** n / math.factorial(2 * n)
    return x * sine / cosine


def hermite_tables(psi):
    t = (lax.broadcasted_iota(jnp.int32, (8, N), 1).astype(F32) - (N - 1) / 2.0) / (N / 48.0)
    previous = math.pow(math.pi, -0.25) * jnp.exp(-0.5 * t * t)
    current = math.sqrt(2.0) * t * previous
    psi[0] = previous
    psi[1] = current
    for n in range(1, ORDERS - 1):
        higher = math.sqrt(2.0 / (n + 1.0)) * t * current - math.sqrt(n / (n + 1.0)) * previous
        psi[n + 1] = higher
        previous, current = current, higher


def spot_profile(index, shape, dim):
    coords = lax.broadcasted_iota(jnp.int32, shape, dim).astype(F32) - (N - 1) / 2.0
    centre = index.astype(F32) - (SPOT_SIDE - 1) / 2.0
    offset = (coords - (N / 40.0) * centre) / (N / 120.0)
    return jnp.exp(-offset * offset)


def split(x):
    high = x.astype(BF16)
    return high, (x - high.astype(F32)).astype(BF16)


def wide(l):
    return slice(l * W, (l + 1) * W)


def beside(x):
    return jnp.concatenate([x[:U], x[U:]], axis=1)


def setup_kernel(plane_id, orders_in, spots_in, left_in, right_in, left, right, source_x, source_y, far_x, far_y,
                 orders, spots, psi, sems):
    mode = plane_id[0]
    pairs = [(orders_in, orders), (spots_in, spots), (left_in, left), (right_in, right)]
    arrivals = [pltpu.make_async_copy(*pair, sems.at[n]) for n, pair in enumerate(pairs)]
    for copy in arrivals:
        copy.start()
    for copy in arrivals[:2]:
        copy.wait()
    hermite_tables(psi)
    row = psi[orders[1, mode]]
    for l in range(4):
        source_y[l] = jnp.concatenate([row[:, lanes(l)]] * 2, axis=1)
    row = AMPLITUDE * psi[orders[0, mode]][0:1]
    for k in range(4):
        source_x[k] = beside(jnp.broadcast_to(row[:, lanes(k)], (B, B)).T)

    for copy in arrivals[2:]:
        copy.wait()
    spot = spots[mode]
    down = spot_profile(spot // SPOT_SIDE, (N, B), 0)
    zero = jnp.zeros((B, B), F32)
    spread = dft4([(down[k * B : (k + 1) * B], zero) for k in range(4)])
    moved = []
    for k in range(4):
        high, low = split(jnp.concatenate(spread[k], axis=0))
        both = dot(left[k], jnp.concatenate([high, low], axis=1))
        total = both[:, :B] + both[:, B:]
        moved.append((total[:B], total[B:]))
    for k, part in enumerate(idft4(moved)):
        far_x[0, k] = beside(part[0]).astype(BF16)
        far_x[1, k] = beside(part[1]).astype(BF16)
    along = spot_profile(spot % SPOT_SIDE, (8, N), 1)
    zero = jnp.zeros((8, B), F32)
    spread = dft4([(along[:, lanes(l)], zero) for l in range(4)])
    moved = []
    for l in range(4):
        high, low = split(jnp.concatenate(spread[l], axis=1))
        both = dot(jnp.concatenate([high, low], axis=0), right[l])
        total = both[:8] + both[8:]
        moved.append((total[:, :B], total[:, B:]))
    for l, y in enumerate(idft4(moved)):
        for c in range(2):
            far_y[c, l] = jnp.concatenate([y[c]] * 2, axis=1)


def setup_call(plane_id, orders, spots, left, right):
    return pl.pallas_call(
        setup_kernel,
        name="setup",
        in_specs=[SMEM, HBM, HBM, HBM, HBM],
        out_specs=[VMEM] * 6,
        out_shape=[
            jax.ShapeDtypeStruct(left.shape, BF16),
            jax.ShapeDtypeStruct(right.shape, BF16),
            jax.ShapeDtypeStruct((4, U, W), F32),
            jax.ShapeDtypeStruct((4, 8, W), F32),
            jax.ShapeDtypeStruct((2, 4, U, W), BF16),
            jax.ShapeDtypeStruct((2, 4, 8, W), F32),
        ],
        scratch_shapes=[
            pltpu.SMEM((2, PLANES), jnp.int32),
            pltpu.SMEM((PLANES,), jnp.int32),
            pltpu.VMEM((ORDERS, 8, N), F32),
            pltpu.SemaphoreType.DMA((4,)),
        ],
        compiler_params=vmem_limit(8),
    )(plane_id, orders, spots, left, right)


def main_kernel(
    plane_id, core_id, side_id, tan_own, *refs,
):
    tan_in, (left, right, source_x, source_y, far_x, far_y, keep, send) = refs[:6], refs[6:14]
    x_ref, v_ref, y_ref, g_ref, mask_ref, tan_ref, grad, sems = refs[14:]
    mode, core, side = plane_id[0], core_id[0], side_id[0]
    pairs = [(tan_own, tan_ref.at[0])]
    for at, (straight, before, after) in ((core, tan_in[:3]), (1 - core, tan_in[3:])):
        across = slice(1, PLANES)
        pairs.append((straight, tan_ref.at[across, at, side]))
        pairs.append((before, tan_ref.at[across, at, 1 - side, 0 : GROUPS // 2]))
        pairs.append((after, tan_ref.at[across, at, 1 - side, GROUPS // 2 : GROUPS]))
    arrivals = [pltpu.make_async_copy(*pair, sems.at[n]) for n, pair in enumerate(pairs)]
    for copy in arrivals:
        copy.start()

    def rows_of(s):
        return slice(s * STRIP, (s + 1) * STRIP)

    def piece_of(k, s):
        return k // 2, (s // 2) * 2, slice((s % 2) * STRIP, (s % 2 + 1) * STRIP)

    def decode(plane, s):
        for k in range(4):
            half, group, rows = piece_of(k, s)
            for l in range(4):
                t = tan_ref[(plane - mode) & 3, half, k % 2, group + l // 2, l % 2, rows].astype(F32)
                twice = 2.0 / (1.0 + t * t)
                mask_ref[plane, 0, k, rows_of(s), wide(l)] = (twice - 1.0).astype(BF16)
                mask_ref[plane, 1, k, rows_of(s), wide(l)] = (twice * t).astype(BF16)

    def load(ref, k, l, s):
        return (ref[0, k, rows_of(s), wide(l)], ref[1, k, rows_of(s), wide(l)])

    def store(ref, k, l, s, x):
        ref[0, k, rows_of(s), wide(l)] = x[0]
        ref[1, k, rows_of(s), wide(l)] = x[1]

    def spread_out(grid, s):
        grid = both_ways(grid, dft4)
        for k in range(4):
            for l in range(4):
                store(x_ref, k, l, s, grid[k][l])

    def gathered_up(s):
        return both_ways([[load(y_ref, k, l, s) for l in range(4)] for k in range(4)], idft4)

    def operate(strip, meanwhile=None):
        for k in range(4):
            cols = []
            for l in range(4):
                parts = [
                    x_ref[c, k, :, l * W + u * B : l * W + (u + 1) * B] for c in range(2) for u in range(2)
                ]
                cols.append(jnp.concatenate(parts, axis=0))
            z = dot(left[k], jnp.concatenate(cols, axis=1))
            for l in range(4):
                v = jnp.concatenate([z[:B, lanes(l)], z[B:, lanes(l)]], axis=1)
                v_ref[l, k * B : (k + 1) * B, :] = v.astype(BF16)
            if meanwhile is not None:
                meanwhile(2 * k)
                meanwhile(2 * k + 1)
        for chunk in range(CHUNKS):
            size = U // CHUNKS
            rows = slice(chunk * size, (chunk + 1) * size)
            for l in range(4):
                parts = [
                    v_ref[l, k * B + u * U + chunk * size : k * B + u * U + (chunk + 1) * size, :]
                    for k in range(4)
                    for u in range(2)
                ]
                y = dot(jnp.concatenate(parts, axis=0), right[l])
                for k in range(4):
                    for c in range(2):
                        at = y[2 * k * size : (2 * k + 2) * size, lanes(c)]
                        both = jnp.concatenate([at[:size], at[size:]], axis=1)
                        y_ref[c, k, rows, wide(l)] = both.astype(BF16)
            if chunk:
                for s in range(STRIPS // CHUNKS):
                    strip((chunk - 1) * (STRIPS // CHUNKS) + s)
        for s in range(STRIPS // CHUNKS):
            strip((CHUNKS - 1) * (STRIPS // CHUNKS) + s)

    def masked(plane, field, k, l, s):
        g = mul(field, load(mask_ref.at[plane], k, l, s))
        store(g_ref.at[plane], k, l, s, g)
        return g

    def first_strip(s):
        decode(0, s)

        def at(k, l):
            field = (source_x[k, rows_of(s), :] * source_y[l, 0:1]).astype(BF16)
            mask = load(mask_ref.at[0], k, l, s)
            g = (field * mask[0], field * mask[1])
            store(g_ref.at[0], k, l, s, g)
            return g

        spread_out([[at(k, l) for l in range(4)] for k in range(4)], s)

    def forward_strip(plane, s):
        field = gathered_up(s)
        spread_out([[masked(plane, field[k][l], k, l, s) for l in range(4)] for k in range(4)], s)

    def last_strip(s):
        field = gathered_up(s)
        for k in range(4):
            a = (far_x[0, k, rows_of(s), :], far_x[1, k, rows_of(s), :])
            for l in range(4):
                part = mul(masked(PLANES - 1, field[k][l], k, l, s), a)
                sums[l] = add(sums[l], (part[0].astype(F32), part[1].astype(F32)))

    def returned(plane, back, k, l, s):
        g = load(g_ref.at[plane], k, l, s)
        half, group, rows = piece_of(k, s)
        grad[half, (k % 2) * GROUPS + group + l // 2, plane, l % 2, rows] = back[0] * g[1] + back[1] * g[0]
        return mul(back, load(mask_ref.at[plane], k, l, s)) if plane else None

    for copy in arrivals:
        copy.wait()
    for s in range(STRIPS):
        first_strip(s)
    for plane in range(1, PLANES - 1):
        operate(functools.partial(forward_strip, plane), functools.partial(decode, plane))
    nothing = jnp.zeros((STRIP, W), F32)
    sums = [(nothing, nothing) for _ in range(4)]
    operate(last_strip, functools.partial(decode, PLANES - 1))
    far = [(far_y[0, l], far_y[1, l]) for l in range(4)]
    total = [mul(s, y) for s, y in zip(sums, far)]
    coupling_re = jnp.sum(sum(t[0] for t in total))
    coupling_im = jnp.sum(sum(t[1] for t in total))
    back_y = [
        (
            (coupling_re * y[0] + coupling_im * y[1]).astype(BF16),
            (coupling_re * y[1] - coupling_im * y[0]).astype(BF16),
        )
        for y in far
    ]

    def turn_strip(s):
        def at(k, l):
            a = (far_x[0, k, rows_of(s), :], far_x[1, k, rows_of(s), :])
            return returned(PLANES - 1, mul(a, back_y[l]), k, l, s)

        spread_out([[at(k, l) for l in range(4)] for k in range(4)], s)

    def backward_strip(plane, s):
        back = gathered_up(s)
        reply = [[returned(plane, back[k][l], k, l, s) for l in range(4)] for k in range(4)]
        if plane:
            spread_out(reply, s)

    for s in range(STRIPS):
        turn_strip(s)
    for plane in reversed(range(PLANES - 1)):
        operate(functools.partial(backward_strip, plane))
    departures = [
        pltpu.make_async_copy(grad.at[1 - core], send, sems.at[0]),
        pltpu.make_async_copy(grad.at[core], keep, sems.at[1]),
    ]
    for copy in departures:
        copy.start()
    for copy in departures:
        copy.wait()


def main_call(plane_id, core_id, side_id, tan_own, tan_in, tables):
    half = (2 * GROUPS, PLANES, 2, *PIECE)
    return pl.pallas_call(
        main_kernel,
        name="modes",
        in_specs=[SMEM] * 3 + [ANY] * 7 + [VMEM] * 6,
        out_specs=[ANY, ANY],
        out_shape=[jax.ShapeDtypeStruct(half, BF16)] * 2,
        scratch_shapes=[
            pltpu.VMEM((2, 4, U, WIDE), BF16),
            pltpu.VMEM((4, N, 2 * B), BF16),
            pltpu.VMEM((2, 4, U, WIDE), BF16),
            pltpu.VMEM((PLANES, 2, 4, U, WIDE), BF16),
            pltpu.VMEM((PLANES, 2, 4, U, WIDE), BF16),
            pltpu.VMEM((PLANES, 2, 2, GROUPS, 2, *PIECE), BF16),
            pltpu.VMEM((2, *half), BF16),
            pltpu.SemaphoreType.DMA((7,)),
        ],
        compiler_params=vmem_limit(26),
    )(plane_id, core_id, side_id, tan_own, *tan_in, *tables)


def tangents_of_strip(phase, first, r, out):
    for u in range(2):
        rows = slice(first + u * U + r * PIECE[0], first + u * U + (r + 1) * PIECE[0])
        for l in range(4):
            out[2 * r + l // 2, l % 2, :, lanes(u)] = half_angle_tangent(phase[rows, lanes(l)]).astype(BF16)


def tangent_kernel(row_id, phase, out, rows, tangents, sems_in, sems_out):
    strips = U // PIECE[0]
    arrivals, departures = [], []
    for r in range(strips):
        for u in range(2):
            at = pl.ds(row_id[0] * B + u * U + r * PIECE[0], PIECE[0])
            here = rows.at[u * U + r * PIECE[0] : u * U + (r + 1) * PIECE[0]]
            arrivals.append(pltpu.make_async_copy(phase.at[0, at], here, sems_in.at[2 * r + u]))
        pair = slice(2 * r, 2 * r + 2)
        departures.append(pltpu.make_async_copy(tangents.at[pair], out.at[pair], sems_out.at[r]))
    for copy in arrivals:
        copy.start()
    for r in range(strips):
        arrivals[2 * r].wait()
        arrivals[2 * r + 1].wait()
        tangents_of_strip(rows, 0, r, tangents)
        departures[r].start()
    for copy in departures:
        copy.wait()


def tangent_call(row_id, phase_masks):
    return pl.pallas_call(
        tangent_kernel,
        name="tangent",
        in_specs=[SMEM, HBM],
        out_specs=HBM,
        out_shape=jax.ShapeDtypeStruct((GROUPS, 2, *PIECE), BF16),
        scratch_shapes=[
            pltpu.VMEM((B, N), F32),
            pltpu.VMEM((GROUPS, 2, *PIECE), BF16),
            pltpu.SemaphoreType.DMA((2 * U // PIECE[0],)),
            pltpu.SemaphoreType.DMA((U // PIECE[0],)),
        ],
        compiler_params=vmem_limit(59),
    )(row_id, phase_masks)


def own_tangent_kernel(phase, out):
    def row(k, carry):
        for r in range(U // PIECE[0]):
            tangents_of_strip(phase.at[0, pl.ds(pl.multiple_of(k * B, B), B)], 0, r, out.at[k // 2, k % 2])
        return carry

    lax.fori_loop(0, 4, row, 0)


def own_tangent_call(phase_masks):
    return pl.pallas_call(
        own_tangent_kernel,
        name="own_tangent",
        in_specs=[VMEM],
        out_specs=VMEM,
        out_shape=jax.ShapeDtypeStruct((2, 2, GROUPS, 2, *PIECE), BF16),
        compiler_params=vmem_limit(6),
    )(phase_masks)


def rows_of_group(half, group, u):
    k, r = 2 * half + group // GROUPS, (group % GROUPS) // 2
    return pl.ds(k * B + u * U + r * PIECE[0], PIECE[0])


def cols_of_group(group, n):
    return lanes(2 * (group % 2) + n)


def finish_kernel(core_id, phase, own, other, out, result, sems):
    squares = jnp.zeros(PIECE, F32)
    for group in range(2 * GROUPS):
        for n in range(2):
            for part in (own, other):
                x = part[group, n].astype(F32)
                squares += x * x
    mean = 4.0 * jnp.sum(squares, keepdims=True) / (N * N)
    scale = -2.0 * lax.rsqrt(mean + EPSILON)
    core = core_id[0]
    departures = []
    for part, half in ((own, core), (other, 1 - core)):
        for side in range(2):
            for group in range(side * GROUPS, (side + 1) * GROUPS):
                for n in range(2):
                    for u in range(2):
                        rows, cols = rows_of_group(half, group, u), cols_of_group(group, n)
                        step = part[group, n, :, lanes(u)].astype(F32) * scale
                        result[rows, cols] = phase[0, rows, cols] + step
            done = pl.ds(pl.multiple_of((2 * half + side) * B, B), B)
            copy = pltpu.make_async_copy(result.at[done], out.at[0, done], sems.at[len(departures)])
            copy.start()
            departures.append(copy)
    for copy in departures:
        copy.wait()


def finish_call(core_id, phase_masks, own, other):
    return pl.pallas_call(
        finish_kernel,
        name="finish",
        in_specs=[SMEM, VMEM, VMEM, VMEM],
        out_specs=HBM,
        out_shape=jax.ShapeDtypeStruct((1, N, N), F32),
        scratch_shapes=[pltpu.VMEM((N, N), F32), pltpu.SemaphoreType.DMA((4,))],
        compiler_params=vmem_limit(8),
    )(core_id, phase_masks, own, other)


def swapped(x):
    return lax.ppermute(x, CORE, [(0, 1), (1, 0)])


def shifted(x, step):
    return lax.ppermute(x, "mode_0", [(i, (i + step) % 4) for i in range(4)])


def from_plane(x, step):
    across = 1 if step == 2 else 0
    here = [(p, z) for p in range(PLANES) for z in range(2)]
    there = [((p + step) % PLANES * 2 + (z ^ across), 2 * p + z) for p, z in here]
    return lax.ppermute(x, Z, there)


def exchanged(x, axes):
    return lax.all_to_all(x, axes, split_axis=0, concat_axis=0, tiled=True)


def from_everyone(x, axes):
    count = lax.axis_size(axes)
    return exchanged(jnp.broadcast_to(x[None], (count, *x.shape)), axes)


def shards(phase_masks, hg_orders, spot_index):
    core_id = lax.axis_index(CORE).astype(jnp.int32)[None]
    plane_id = lax.axis_index("plane").astype(jnp.int32)[None]
    side_id = (lax.axis_index("mode_0").astype(jnp.int32) & 1)[None]
    tangent = tangent_call(2 * core_id + side_id, phase_masks)
    arriving = [from_plane(tangent, step) for step in (1, 2, -1)]
    tan_own = own_tangent_call(phase_masks)
    tables = setup_call(plane_id, hg_orders.T, spot_index, *block_operators())
    arrived, tan_own, tables = lax.optimization_barrier((arriving, tan_own, tables))
    straight = jnp.stack(arrived)
    before = shifted(straight[:, : GROUPS // 2], 1)
    after = shifted(straight[:, GROUPS // 2 :], -1)
    half_own = [straight, before, after]
    tan_in = half_own + [swapped(x) for x in half_own]
    keep, send = main_call(plane_id, core_id, side_id, tan_own, tan_in, tables)
    pair = keep + swapped(send)
    column = jnp.sum(exchanged(pair, XY).astype(F32), axis=0).astype(BF16)
    pieces = column.reshape(2 * PLANES, *PIECE)
    total = jnp.sum(exchanged(pieces, Z).astype(F32), axis=0).astype(BF16)
    own = from_everyone(total, CHIPS).reshape(2 * GROUPS, 2, *PIECE)
    other = swapped(own)
    return finish_call(core_id, phase_masks, own, other)


def solution(mesh):
    finer = Mesh(
        mesh.devices.reshape(mesh.shape["plane"], 4, 4, 2, 2),
        ("plane", "mode_0", "mode_1", "mode_2", "mode_3"),
    )
    placed = (P("plane", None, None), P(MODE, None), P(MODE))
    return jax.shard_map(
        shards, mesh=finer, in_specs=placed, out_specs=P("plane", None, None), check_vma=False
    )
```

```python
import functools
import math

import jax
import jax.numpy as jnp
import numpy as np
from jax import lax
from jax.experimental import pallas as pl
from jax.experimental.pallas import tpu as pltpu
from jax.sharding import Mesh
from jax.sharding import PartitionSpec as P

ORDERS = 45
SPOT_SIDE = 32
MODE = ("mode_0", "mode_1", "mode_2", "mode_3")
XY = ("mode_0", "mode_1")
Z = ("plane", "mode_2")
CORE = "mode_3"
PLANES = 4
N = 512
B = 128
U = B // 2
W = 2 * B
WIDE = 4 * W
STRIP = 8
STRIPS = U // STRIP
CHUNKS = 4
PIECE = (16, W)
GROUPS = 8
CHIRP_RATE = math.pi / 48.0 * (math.pi / 48.0)
AMPLITUDE = 12.0
EPSILON = 1e-06
F32 = jnp.float32
BF16 = jnp.bfloat16
SMEM = pl.BlockSpec(memory_space=pltpu.SMEM)
VMEM = pl.BlockSpec(memory_space=pltpu.VMEM)
ANY = pl.BlockSpec(memory_space=pl.ANY)
HBM = pl.BlockSpec(memory_space=pltpu.HBM)


def vmem_limit(mib):
    return pltpu.CompilerParams(vmem_limit_bytes=mib << 20)


def block_operators():
    f = np.arange(N)
    s = (f + N // 2) % N - N // 2
    chirp = np.exp(-1j * CHIRP_RATE * s.astype(np.float64) ** 2)
    phase = np.exp(2j * np.pi * ((f[:, None] * f[None, :]) % N) / N)
    kernel = (phase * chirp[None, :]).sum(axis=1) / N
    offset = np.arange(B)[:, None] - np.arange(B)[None, :]
    left, right = [], []
    for k in range(4):
        block = sum((-1j) ** (k * m) * kernel[(offset + B * m) % N] for m in range(4)) / 4.0
        real = np.block([[block.real, -block.imag], [block.imag, block.real]])
        left.append(real)
        right.append(real.T)
    to = lambda x: jnp.asarray(np.stack(x).astype(np.float32)).astype(BF16)
    return to(left), to(right)


def add(x, y):
    return (x[0] + y[0], x[1] + y[1])


def sub(x, y):
    return (x[0] - y[0], x[1] - y[1])


def turned(x, y):
    return (x[0] - y[1], x[1] + y[0])


def turned_back(x, y):
    return (x[0] + y[1], x[1] - y[0])


def dft4(x):
    a, b, c, d = add(x[0], x[2]), sub(x[0], x[2]), add(x[1], x[3]), sub(x[1], x[3])
    return [add(a, c), turned_back(b, d), sub(a, c), turned(b, d)]


def idft4(x):
    a, b, c, d = add(x[0], x[2]), sub(x[0], x[2]), add(x[1], x[3]), sub(x[1], x[3])
    return [add(a, c), turned(b, d), sub(a, c), turned_back(b, d)]


def both_ways(grid, transform):
    grid = [transform(row) for row in grid]
    cols = [transform([grid[k][l] for k in range(4)]) for l in range(4)]
    return [[cols[l][k] for l in range(4)] for k in range(4)]


def mul(x, y):
    return (x[0] * y[0] - x[1] * y[1], x[0] * y[1] + x[1] * y[0])


def dot(a, b):
    return jnp.dot(a, b, preferred_element_type=F32)


def lanes(l):
    return slice(l * B, (l + 1) * B)


def half_angle_tangent(phase):
    x = 0.5 * phase
    y = x * x
    sine, cosine = 0.0, 0.0
    for n in reversed(range(7)):
        sine = sine * y + (-1) ** n / math.factorial(2 * n + 1)
        cosine = cosine * y + (-1) ** n / math.factorial(2 * n)
    return x * sine / cosine


def hermite_tables(psi):
    t = (lax.broadcasted_iota(jnp.int32, (8, N), 1).astype(F32) - (N - 1) / 2.0) / (N / 48.0)
    previous = math.pow(math.pi, -0.25) * jnp.exp(-0.5 * t * t)
    current = math.sqrt(2.0) * t * previous
    psi[0] = previous
    psi[1] = current
    for n in range(1, ORDERS - 1):
        higher = math.sqrt(2.0 / (n + 1.0)) * t * current - math.sqrt(n / (n + 1.0)) * previous
        psi[n + 1] = higher
        previous, current = current, higher


def spot_profile(index, shape, dim):
    coords = lax.broadcasted_iota(jnp.int32, shape, dim).astype(F32) - (N - 1) / 2.0
    centre = index.astype(F32) - (SPOT_SIDE - 1) / 2.0
    offset = (coords - (N / 40.0) * centre) / (N / 120.0)
    return jnp.exp(-offset * offset)


def split(x):
    high = x.astype(BF16)
    return high, (x - high.astype(F32)).astype(BF16)


def wide(l):
    return slice(l * W, (l + 1) * W)


def beside(x):
    return jnp.concatenate([x[:U], x[U:]], axis=1)


def setup_kernel(plane_id, orders_in, spots_in, left_in, right_in, left, right, source_x, source_y, far_x, far_y,
                 orders, spots, psi, sems):
    mode = plane_id[0]
    pairs = [(orders_in, orders), (spots_in, spots), (left_in, left), (right_in, right)]
    arrivals = [pltpu.make_async_copy(*pair, sems.at[n]) for n, pair in enumerate(pairs)]
    for copy in arrivals:
        copy.start()
    for copy in arrivals[:2]:
        copy.wait()
    hermite_tables(psi)
    row = psi[orders[1, mode]]
    for l in range(4):
        source_y[l] = jnp.concatenate([row[:, lanes(l)]] * 2, axis=1)
    row = AMPLITUDE * psi[orders[0, mode]][0:1]
    for k in range(4):
        source_x[k] = beside(jnp.broadcast_to(row[:, lanes(k)], (B, B)).T)

    for copy in arrivals[2:]:
        copy.wait()
    spot = spots[mode]
    down = spot_profile(spot // SPOT_SIDE, (N, B), 0)
    zero = jnp.zeros((B, B), F32)
    spread = dft4([(down[k * B : (k + 1) * B], zero) for k in range(4)])
    moved = []
    for k in range(4):
        high, low = split(jnp.concatenate(spread[k], axis=0))
        both = dot(left[k], jnp.concatenate([high, low], axis=1))
        total = both[:, :B] + both[:, B:]
        moved.append((total[:B], total[B:]))
    for k, part in enumerate(idft4(moved)):
        far_x[0, k] = beside(part[0]).astype(BF16)
        far_x[1, k] = beside(part[1]).astype(BF16)
    along = spot_profile(spot % SPOT_SIDE, (8, N), 1)
    zero = jnp.zeros((8, B), F32)
    spread = dft4([(along[:, lanes(l)], zero) for l in range(4)])
    moved = []
    for l in range(4):
        high, low = split(jnp.concatenate(spread[l], axis=1))
        both = dot(jnp.concatenate([high, low], axis=0), right[l])
        total = both[:8] + both[8:]
        moved.append((total[:, :B], total[:, B:]))
    for l, y in enumerate(idft4(moved)):
        for c in range(2):
            far_y[c, l] = jnp.concatenate([y[c]] * 2, axis=1)


def setup_call(plane_id, orders, spots, left, right):
    return pl.pallas_call(
        setup_kernel,
        name="setup",
        in_specs=[SMEM, HBM, HBM, HBM, HBM],
        out_specs=[VMEM] * 6,
        out_shape=[
            jax.ShapeDtypeStruct(left.shape, BF16),
            jax.ShapeDtypeStruct(right.shape, BF16),
            jax.ShapeDtypeStruct((4, U, W), F32),
            jax.ShapeDtypeStruct((4, 8, W), F32),
            jax.ShapeDtypeStruct((2, 4, U, W), BF16),
            jax.ShapeDtypeStruct((2, 4, 8, W), F32),
        ],
        scratch_shapes=[
            pltpu.SMEM((2, PLANES), jnp.int32),
            pltpu.SMEM((PLANES,), jnp.int32),
            pltpu.VMEM((ORDERS, 8, N), F32),
            pltpu.SemaphoreType.DMA((4,)),
        ],
        compiler_params=vmem_limit(8),
    )(plane_id, orders, spots, left, right)


def main_kernel(
    plane_id, core_id, side_id, tan_own, *refs,
):
    tan_in, (left, right, source_x, source_y, far_x, far_y, keep, send) = refs[:12], refs[12:20]
    x_ref, v_ref, y_ref, g_ref, mask_ref, tan_ref, grad, sems = refs[20:]
    mode, core, side = plane_id[0], core_id[0], side_id[0]
    pairs = [(tan_own, tan_ref.at[0])]
    for n, (straight, before, after) in enumerate(zip(tan_in[::3], tan_in[1::3], tan_in[2::3])):
        at = core if n < 2 else 1 - core
        across = 3 if n % 2 else slice(1, 3)
        pairs.append((straight, tan_ref.at[across, at, side]))
        pairs.append((before, tan_ref.at[across, at, 1 - side, 0 : GROUPS // 2]))
        pairs.append((after, tan_ref.at[across, at, 1 - side, GROUPS // 2 : GROUPS]))
    arrivals = [pltpu.make_async_copy(*pair, sems.at[n]) for n, pair in enumerate(pairs)]
    for copy in arrivals:
        copy.start()

    def rows_of(s):
        return slice(s * STRIP, (s + 1) * STRIP)

    def piece_of(k, s):
        return k // 2, (s // 2) * 2, slice((s % 2) * STRIP, (s % 2 + 1) * STRIP)

    def decode(plane, s):
        distance = (plane - mode) & 3
        slot = distance ^ (distance >> 1)
        for k in range(4):
            half, group, rows = piece_of(k, s)
            for l in range(4):
                t = tan_ref[slot, half, k % 2, group + l // 2, l % 2, rows].astype(F32)
                twice = 2.0 / (1.0 + t * t)
                mask_ref[plane, 0, k, rows_of(s), wide(l)] = (twice - 1.0).astype(BF16)
                mask_ref[plane, 1, k, rows_of(s), wide(l)] = (twice * t).astype(BF16)

    def load(ref, k, l, s):
        return (ref[0, k, rows_of(s), wide(l)], ref[1, k, rows_of(s), wide(l)])

    def store(ref, k, l, s, x):
        ref[0, k, rows_of(s), wide(l)] = x[0]
        ref[1, k, rows_of(s), wide(l)] = x[1]

    def spread_out(grid, s):
        grid = both_ways(grid, dft4)
        for k in range(4):
            for l in range(4):
                store(x_ref, k, l, s, grid[k][l])

    def gathered_up(s):
        return both_ways([[load(y_ref, k, l, s) for l in range(4)] for k in range(4)], idft4)

    def operate(strip, meanwhile=None):
        for k in range(4):
            cols = []
            for l in range(4):
                parts = [
                    x_ref[c, k, :, l * W + u * B : l * W + (u + 1) * B] for c in range(2) for u in range(2)
                ]
                cols.append(jnp.concatenate(parts, axis=0))
            z = dot(left[k], jnp.concatenate(cols, axis=1))
            for l in range(4):
                v = jnp.concatenate([z[:B, lanes(l)], z[B:, lanes(l)]], axis=1)
                v_ref[l, k * B : (k + 1) * B, :] = v.astype(BF16)
            if meanwhile is not None:
                meanwhile(2 * k)
                meanwhile(2 * k + 1)
        for chunk in range(CHUNKS):
            size = U // CHUNKS
            rows = slice(chunk * size, (chunk + 1) * size)
            for l in range(4):
                parts = [
                    v_ref[l, k * B + u * U + chunk * size : k * B + u * U + (chunk + 1) * size, :]
                    for k in range(4)
                    for u in range(2)
                ]
                y = dot(jnp.concatenate(parts, axis=0), right[l])
                for k in range(4):
                    for c in range(2):
                        at = y[2 * k * size : (2 * k + 2) * size, lanes(c)]
                        both = jnp.concatenate([at[:size], at[size:]], axis=1)
                        y_ref[c, k, rows, wide(l)] = both.astype(BF16)
            if chunk:
                for s in range(STRIPS // CHUNKS):
                    strip((chunk - 1) * (STRIPS // CHUNKS) + s)
        for s in range(STRIPS // CHUNKS):
            strip((CHUNKS - 1) * (STRIPS // CHUNKS) + s)

    def masked(plane, field, k, l, s):
        g = mul(field, load(mask_ref.at[plane], k, l, s))
        store(g_ref.at[plane], k, l, s, g)
        return g

    def first_strip(s):
        decode(0, s)

        def at(k, l):
            field = (source_x[k, rows_of(s), :] * source_y[l, 0:1]).astype(BF16)
            mask = load(mask_ref.at[0], k, l, s)
            g = (field * mask[0], field * mask[1])
            store(g_ref.at[0], k, l, s, g)
            return g

        spread_out([[at(k, l) for l in range(4)] for k in range(4)], s)

    def forward_strip(plane, s):
        field = gathered_up(s)
        spread_out([[masked(plane, field[k][l], k, l, s) for l in range(4)] for k in range(4)], s)

    def last_strip(s):
        field = gathered_up(s)
        for k in range(4):
            a = (far_x[0, k, rows_of(s), :], far_x[1, k, rows_of(s), :])
            for l in range(4):
                part = mul(masked(PLANES - 1, field[k][l], k, l, s), a)
                sums[l] = add(sums[l], (part[0].astype(F32), part[1].astype(F32)))

    def returned(plane, back, k, l, s):
        g = load(g_ref.at[plane], k, l, s)
        half, group, rows = piece_of(k, s)
        grad[half, (k % 2) * GROUPS + group + l // 2, plane, l % 2, rows] = back[0] * g[1] + back[1] * g[0]
        return mul(back, load(mask_ref.at[plane], k, l, s)) if plane else None

    for copy in arrivals:
        copy.wait()
    for s in range(STRIPS):
        first_strip(s)
    for plane in range(1, PLANES - 1):
        operate(functools.partial(forward_strip, plane), functools.partial(decode, plane))
    nothing = jnp.zeros((STRIP, W), F32)
    sums = [(nothing, nothing) for _ in range(4)]
    operate(last_strip, functools.partial(decode, PLANES - 1))
    far = [(far_y[0, l], far_y[1, l]) for l in range(4)]
    total = [mul(s, y) for s, y in zip(sums, far)]
    coupling_re = jnp.sum(sum(t[0] for t in total))
    coupling_im = jnp.sum(sum(t[1] for t in total))
    back_y = [
        (
            (coupling_re * y[0] + coupling_im * y[1]).astype(BF16),
            (coupling_re * y[1] - coupling_im * y[0]).astype(BF16),
        )
        for y in far
    ]

    def turn_strip(s):
        def at(k, l):
            a = (far_x[0, k, rows_of(s), :], far_x[1, k, rows_of(s), :])
            return returned(PLANES - 1, mul(a, back_y[l]), k, l, s)

        spread_out([[at(k, l) for l in range(4)] for k in range(4)], s)

    def backward_strip(plane, s):
        back = gathered_up(s)
        reply = [[returned(plane, back[k][l], k, l, s) for l in range(4)] for k in range(4)]
        if plane:
            spread_out(reply, s)

    for s in range(STRIPS):
        turn_strip(s)
    for plane in reversed(range(PLANES - 1)):
        operate(functools.partial(backward_strip, plane))
    departures = [
        pltpu.make_async_copy(grad.at[1 - core], send, sems.at[0]),
        pltpu.make_async_copy(grad.at[core], keep, sems.at[1]),
    ]
    for copy in departures:
        copy.start()
    for copy in departures:
        copy.wait()


def main_call(plane_id, core_id, side_id, tan_own, tan_in, tables):
    half = (2 * GROUPS, PLANES, 2, *PIECE)
    return pl.pallas_call(
        main_kernel,
        name="modes",
        in_specs=[SMEM] * 3 + [ANY] * 13 + [VMEM] * 6,
        out_specs=[ANY, ANY],
        out_shape=[jax.ShapeDtypeStruct(half, BF16)] * 2,
        scratch_shapes=[
            pltpu.VMEM((2, 4, U, WIDE), BF16),
            pltpu.VMEM((4, N, 2 * B), BF16),
            pltpu.VMEM((2, 4, U, WIDE), BF16),
            pltpu.VMEM((PLANES, 2, 4, U, WIDE), BF16),
            pltpu.VMEM((PLANES, 2, 4, U, WIDE), BF16),
            pltpu.VMEM((PLANES, 2, 2, GROUPS, 2, *PIECE), BF16),
            pltpu.VMEM((2, *half), BF16),
            pltpu.SemaphoreType.DMA((13,)),
        ],
        compiler_params=vmem_limit(26),
    )(plane_id, core_id, side_id, tan_own, *tan_in, *tables)


def tangents_of_strip(phase, first, r, out):
    for u in range(2):
        rows = slice(first + u * U + r * PIECE[0], first + u * U + (r + 1) * PIECE[0])
        for l in range(4):
            out[2 * r + l // 2, l % 2, :, lanes(u)] = half_angle_tangent(phase[rows, lanes(l)]).astype(BF16)


def tangent_kernel(row_id, phase, out, rows, tangents, sems_in, sems_out):
    strips = U // PIECE[0]
    arrivals, departures = [], []
    for r in range(strips):
        for u in range(2):
            at = pl.ds(row_id[0] * B + u * U + r * PIECE[0], PIECE[0])
            here = rows.at[u * U + r * PIECE[0] : u * U + (r + 1) * PIECE[0]]
            arrivals.append(pltpu.make_async_copy(phase.at[0, at], here, sems_in.at[2 * r + u]))
        pair = slice(2 * r, 2 * r + 2)
        departures.append(pltpu.make_async_copy(tangents.at[pair], out.at[pair], sems_out.at[r]))
    for copy in arrivals:
        copy.start()
    for r in range(strips):
        arrivals[2 * r].wait()
        arrivals[2 * r + 1].wait()
        tangents_of_strip(rows, 0, r, tangents)
        departures[r].start()
    for copy in departures:
        copy.wait()


def tangent_call(row_id, phase_masks):
    return pl.pallas_call(
        tangent_kernel,
        name="tangent",
        in_specs=[SMEM, HBM],
        out_specs=HBM,
        out_shape=jax.ShapeDtypeStruct((GROUPS, 2, *PIECE), BF16),
        scratch_shapes=[
            pltpu.VMEM((B, N), F32),
            pltpu.VMEM((GROUPS, 2, *PIECE), BF16),
            pltpu.SemaphoreType.DMA((2 * U // PIECE[0],)),
            pltpu.SemaphoreType.DMA((U // PIECE[0],)),
        ],
        compiler_params=vmem_limit(59),
    )(row_id, phase_masks)


def own_tangent_kernel(phase, out):
    def row(k, carry):
        for r in range(U // PIECE[0]):
            tangents_of_strip(phase.at[0, pl.ds(pl.multiple_of(k * B, B), B)], 0, r, out.at[k // 2, k % 2])
        return carry

    lax.fori_loop(0, 4, row, 0)


def own_tangent_call(phase_masks):
    return pl.pallas_call(
        own_tangent_kernel,
        name="own_tangent",
        in_specs=[VMEM],
        out_specs=VMEM,
        out_shape=jax.ShapeDtypeStruct((2, 2, GROUPS, 2, *PIECE), BF16),
        compiler_params=vmem_limit(6),
    )(phase_masks)


def rows_of_group(half, group, u):
    k, r = 2 * half + group // GROUPS, (group % GROUPS) // 2
    return pl.ds(k * B + u * U + r * PIECE[0], PIECE[0])


def cols_of_group(group, n):
    return lanes(2 * (group % 2) + n)


def finish_kernel(core_id, phase, own, other, out, result, sems):
    squares = jnp.zeros(PIECE, F32)
    for group in range(2 * GROUPS):
        for n in range(2):
            for part in (own, other):
                x = part[group, n].astype(F32)
                squares += x * x
    mean = 4.0 * jnp.sum(squares, keepdims=True) / (N * N)
    scale = -2.0 * lax.rsqrt(mean + EPSILON)
    core = core_id[0]
    departures = []
    for part, half in ((own, core), (other, 1 - core)):
        for side in range(2):
            for group in range(side * GROUPS, (side + 1) * GROUPS):
                for n in range(2):
                    for u in range(2):
                        rows, cols = rows_of_group(half, group, u), cols_of_group(group, n)
                        step = part[group, n, :, lanes(u)].astype(F32) * scale
                        result[rows, cols] = phase[0, rows, cols] + step
            done = pl.ds(pl.multiple_of((2 * half + side) * B, B), B)
            copy = pltpu.make_async_copy(result.at[done], out.at[0, done], sems.at[len(departures)])
            copy.start()
            departures.append(copy)
    for copy in departures:
        copy.wait()


def finish_call(core_id, phase_masks, own, other):
    return pl.pallas_call(
        finish_kernel,
        name="finish",
        in_specs=[SMEM, VMEM, VMEM, VMEM],
        out_specs=HBM,
        out_shape=jax.ShapeDtypeStruct((1, N, N), F32),
        scratch_shapes=[pltpu.VMEM((N, N), F32), pltpu.SemaphoreType.DMA((4,))],
        compiler_params=vmem_limit(8),
    )(core_id, phase_masks, own, other)


def swapped(x):
    return lax.ppermute(x, CORE, [(0, 1), (1, 0)])


def shifted(x, step):
    return lax.ppermute(x, "mode_0", [(i, (i + step) % 4) for i in range(4)])


def from_plane(x, step):
    across = 1 if step == 2 else 0
    here = [(p, z) for p in range(PLANES) for z in range(2)]
    there = [((p + step) % PLANES * 2 + (z ^ across), 2 * p + z) for p, z in here]
    return lax.ppermute(x, Z, there)


def exchanged(x, axes):
    return lax.all_to_all(x, axes, split_axis=0, concat_axis=0, tiled=True)


def from_everyone(x, axes):
    count = lax.axis_size(axes)
    return exchanged(jnp.broadcast_to(x[None], (count, *x.shape)), axes)


def shards(phase_masks, hg_orders, spot_index):
    core_id = lax.axis_index(CORE).astype(jnp.int32)[None]
    plane_id = lax.axis_index("plane").astype(jnp.int32)[None]
    side_id = (lax.axis_index("mode_0").astype(jnp.int32) & 1)[None]
    tangent = tangent_call(2 * core_id + side_id, phase_masks)
    beside_own = [from_plane(tangent, step) for step in (1, -1)]
    opposite = from_plane(tangent, 2)
    tan_own = own_tangent_call(phase_masks)
    tables = setup_call(plane_id, hg_orders.T, spot_index, *block_operators())
    beside_own, tan_own, tables = lax.optimization_barrier((beside_own, tan_own, tables))
    beside_own = jnp.stack(beside_own)
    cut = GROUPS // 2
    half_own = [beside_own, shifted(beside_own[:, :cut], 1), shifted(beside_own[:, cut:], -1)]
    half_own += [opposite, shifted(opposite[:cut], 1), shifted(opposite[cut:], -1)]
    tan_in = half_own + [swapped(x) for x in half_own]
    keep, send = main_call(plane_id, core_id, side_id, tan_own, tan_in, tables)
    pair = keep + swapped(send)
    column = jnp.sum(exchanged(pair, XY).astype(F32), axis=0).astype(BF16)
    pieces = jnp.repeat(column, 2, axis=0)
    total = jnp.sum(exchanged(pieces, Z).astype(F32), axis=0).astype(BF16)
    own = from_everyone(total, XY)
    other = swapped(own)
    return finish_call(core_id, phase_masks, own, other)


def solution(mesh):
    finer = Mesh(
        mesh.devices.reshape(mesh.shape["plane"], 4, 4, 2, 2),
        ("plane", "mode_0", "mode_1", "mode_2", "mode_3"),
    )
    placed = (P("plane", None, None), P(MODE, None), P(MODE))
    return jax.shard_map(
        shards, mesh=finer, in_specs=placed, out_specs=P("plane", None, None), check_vma=False
    )
```

```python
import functools
import math

import jax
import jax.numpy as jnp
import numpy as np
from jax import lax
from jax.experimental import pallas as pl
from jax.experimental.pallas import tpu as pltpu
from jax.sharding import Mesh
from jax.sharding import PartitionSpec as P

ORDERS = 45
SPOT_SIDE = 32
MODE = ("mode_0", "mode_1", "mode_2", "mode_3")
XY = ("mode_0", "mode_1")
Z = ("plane", "mode_2")
CORE = "mode_3"
PLANES = 4
N = 512
B = 128
U = B // 2
W = 2 * B
WIDE = 4 * W
STRIP = 8
STRIPS = U // STRIP
CHUNKS = 4
PIECE = (16, W)
GROUPS = 8
CHIRP_RATE = math.pi / 48.0 * (math.pi / 48.0)
AMPLITUDE = 12.0
EPSILON = 1e-06
F32 = jnp.float32
BF16 = jnp.bfloat16
SMEM = pl.BlockSpec(memory_space=pltpu.SMEM)
VMEM = pl.BlockSpec(memory_space=pltpu.VMEM)
ANY = pl.BlockSpec(memory_space=pl.ANY)
HBM = pl.BlockSpec(memory_space=pltpu.HBM)


def vmem_limit(mib):
    return pltpu.CompilerParams(vmem_limit_bytes=mib << 20)


def block_operators():
    f = np.arange(N)
    s = (f + N // 2) % N - N // 2
    chirp = np.exp(-1j * CHIRP_RATE * s.astype(np.float64) ** 2)
    phase = np.exp(2j * np.pi * ((f[:, None] * f[None, :]) % N) / N)
    kernel = (phase * chirp[None, :]).sum(axis=1) / N
    offset = np.arange(B)[:, None] - np.arange(B)[None, :]
    left, right = [], []
    for k in range(4):
        block = sum((-1j) ** (k * m) * kernel[(offset + B * m) % N] for m in range(4)) / 4.0
        real = np.block([[block.real, -block.imag], [block.imag, block.real]])
        left.append(real)
        right.append(real.T)
    to = lambda x: jnp.asarray(np.stack(x).astype(np.float32)).astype(BF16)
    return to(left), to(right)


def add(x, y):
    return (x[0] + y[0], x[1] + y[1])


def sub(x, y):
    return (x[0] - y[0], x[1] - y[1])


def turned(x, y):
    return (x[0] - y[1], x[1] + y[0])


def turned_back(x, y):
    return (x[0] + y[1], x[1] - y[0])


def dft4(x):
    a, b, c, d = add(x[0], x[2]), sub(x[0], x[2]), add(x[1], x[3]), sub(x[1], x[3])
    return [add(a, c), turned_back(b, d), sub(a, c), turned(b, d)]


def idft4(x):
    a, b, c, d = add(x[0], x[2]), sub(x[0], x[2]), add(x[1], x[3]), sub(x[1], x[3])
    return [add(a, c), turned(b, d), sub(a, c), turned_back(b, d)]


def both_ways(grid, transform):
    grid = [transform(row) for row in grid]
    cols = [transform([grid[k][l] for k in range(4)]) for l in range(4)]
    return [[cols[l][k] for l in range(4)] for k in range(4)]


def mul(x, y):
    return (x[0] * y[0] - x[1] * y[1], x[0] * y[1] + x[1] * y[0])


def dot(a, b):
    return jnp.dot(a, b, preferred_element_type=F32)


def lanes(l):
    return slice(l * B, (l + 1) * B)


def half_angle_tangent(phase):
    x = 0.5 * phase
    y = x * x
    sine, cosine = 0.0, 0.0
    for n in reversed(range(7)):
        sine = sine * y + (-1) ** n / math.factorial(2 * n + 1)
        cosine = cosine * y + (-1) ** n / math.factorial(2 * n)
    return x * sine / cosine


def hermite_tables(psi):
    t = (lax.broadcasted_iota(jnp.int32, (8, N), 1).astype(F32) - (N - 1) / 2.0) / (N / 48.0)
    previous = math.pow(math.pi, -0.25) * jnp.exp(-0.5 * t * t)
    current = math.sqrt(2.0) * t * previous
    psi[0] = previous
    psi[1] = current
    for n in range(1, ORDERS - 1):
        higher = math.sqrt(2.0 / (n + 1.0)) * t * current - math.sqrt(n / (n + 1.0)) * previous
        psi[n + 1] = higher
        previous, current = current, higher


def spot_profile(index, shape, dim):
    coords = lax.broadcasted_iota(jnp.int32, shape, dim).astype(F32) - (N - 1) / 2.0
    centre = index.astype(F32) - (SPOT_SIDE - 1) / 2.0
    offset = (coords - (N / 40.0) * centre) / (N / 120.0)
    return jnp.exp(-offset * offset)


def split(x):
    high = x.astype(BF16)
    return high, (x - high.astype(F32)).astype(BF16)


def wide(l):
    return slice(l * W, (l + 1) * W)


def beside(x):
    return jnp.concatenate([x[:U], x[U:]], axis=1)


def setup_kernel(plane_id, orders_in, spots_in, left_in, right_in, left, right, source_x, source_y, far_x, far_y,
                 orders, spots, psi, sems):
    mode = plane_id[0]
    pairs = [(orders_in, orders), (spots_in, spots), (left_in, left), (right_in, right)]
    arrivals = [pltpu.make_async_copy(*pair, sems.at[n]) for n, pair in enumerate(pairs)]
    for copy in arrivals:
        copy.start()
    for copy in arrivals[:2]:
        copy.wait()
    hermite_tables(psi)
    row = psi[orders[1, mode]]
    for l in range(4):
        source_y[l] = jnp.concatenate([row[:, lanes(l)]] * 2, axis=1)
    row = AMPLITUDE * psi[orders[0, mode]][0:1]
    for k in range(4):
        source_x[k] = beside(jnp.broadcast_to(row[:, lanes(k)], (B, B)).T)

    for copy in arrivals[2:]:
        copy.wait()
    spot = spots[mode]
    down = spot_profile(spot // SPOT_SIDE, (N, B), 0)
    zero = jnp.zeros((B, B), F32)
    spread = dft4([(down[k * B : (k + 1) * B], zero) for k in range(4)])
    moved = []
    for k in range(4):
        high, low = split(jnp.concatenate(spread[k], axis=0))
        both = dot(left[k], jnp.concatenate([high, low], axis=1))
        total = both[:, :B] + both[:, B:]
        moved.append((total[:B], total[B:]))
    for k, part in enumerate(idft4(moved)):
        far_x[0, k] = beside(part[0]).astype(BF16)
        far_x[1, k] = beside(part[1]).astype(BF16)
    along = spot_profile(spot % SPOT_SIDE, (8, N), 1)
    zero = jnp.zeros((8, B), F32)
    spread = dft4([(along[:, lanes(l)], zero) for l in range(4)])
    moved = []
    for l in range(4):
        high, low = split(jnp.concatenate(spread[l], axis=1))
        both = dot(jnp.concatenate([high, low], axis=0), right[l])
        total = both[:8] + both[8:]
        moved.append((total[:, :B], total[:, B:]))
    for l, y in enumerate(idft4(moved)):
        for c in range(2):
            far_y[c, l] = jnp.concatenate([y[c]] * 2, axis=1)


def setup_call(plane_id, orders, spots, left, right):
    return pl.pallas_call(
        setup_kernel,
        name="setup",
        in_specs=[SMEM, HBM, HBM, HBM, HBM],
        out_specs=[VMEM] * 6,
        out_shape=[
            jax.ShapeDtypeStruct(left.shape, BF16),
            jax.ShapeDtypeStruct(right.shape, BF16),
            jax.ShapeDtypeStruct((4, U, W), F32),
            jax.ShapeDtypeStruct((4, 8, W), F32),
            jax.ShapeDtypeStruct((2, 4, U, W), BF16),
            jax.ShapeDtypeStruct((2, 4, 8, W), F32),
        ],
        scratch_shapes=[
            pltpu.SMEM((2, PLANES), jnp.int32),
            pltpu.SMEM((PLANES,), jnp.int32),
            pltpu.VMEM((ORDERS, 8, N), F32),
            pltpu.SemaphoreType.DMA((4,)),
        ],
        compiler_params=vmem_limit(8),
    )(plane_id, orders, spots, left, right)


def main_kernel(
    plane_id, core_id, side_id, tan_own, *refs,
):
    tan_in, (left, right, source_x, source_y, far_x, far_y, keep, send) = refs[:12], refs[12:20]
    x_ref, v_ref, y_ref, g_ref, mask_ref, tan_ref, grad, sems = refs[20:]
    mode, core, side = plane_id[0], core_id[0], side_id[0]
    tan_ref[0] = tan_own[...]
    cut = GROUPS // 2
    for n, (straight, before, after) in enumerate(zip(tan_in[::3], tan_in[1::3], tan_in[2::3])):
        at = core if n < 2 else 1 - core
        across = 3 if n % 2 else slice(1, 3)
        tan_ref[across, at, side] = straight[...]
        tan_ref[across, at, 1 - side, 0:cut] = before[...]
        tan_ref[across, at, 1 - side, cut:GROUPS] = after[...]

    def rows_of(s):
        return slice(s * STRIP, (s + 1) * STRIP)

    def piece_of(k, s):
        return k // 2, (s // 2) * 2, slice((s % 2) * STRIP, (s % 2 + 1) * STRIP)

    def decode(plane, s):
        distance = (plane - mode) & 3
        slot = distance ^ (distance >> 1)
        for k in range(4):
            half, group, rows = piece_of(k, s)
            for l in range(4):
                t = tan_ref[slot, half, k % 2, group + l // 2, l % 2, rows].astype(F32)
                twice = 2.0 / (1.0 + t * t)
                mask_ref[plane, 0, k, rows_of(s), wide(l)] = (twice - 1.0).astype(BF16)
                mask_ref[plane, 1, k, rows_of(s), wide(l)] = (twice * t).astype(BF16)

    def load(ref, k, l, s):
        return (ref[0, k, rows_of(s), wide(l)], ref[1, k, rows_of(s), wide(l)])

    def store(ref, k, l, s, x):
        ref[0, k, rows_of(s), wide(l)] = x[0]
        ref[1, k, rows_of(s), wide(l)] = x[1]

    def spread_out(grid, s):
        grid = both_ways(grid, dft4)
        for k in range(4):
            for l in range(4):
                store(x_ref, k, l, s, grid[k][l])

    def gathered_up(s):
        return both_ways([[load(y_ref, k, l, s) for l in range(4)] for k in range(4)], idft4)

    def operate(strip, meanwhile=None):
        for k in range(4):
            cols = []
            for l in range(4):
                parts = [
                    x_ref[c, k, :, l * W + u * B : l * W + (u + 1) * B] for c in range(2) for u in range(2)
                ]
                cols.append(jnp.concatenate(parts, axis=0))
            z = dot(left[k], jnp.concatenate(cols, axis=1))
            for l in range(4):
                v = jnp.concatenate([z[:B, lanes(l)], z[B:, lanes(l)]], axis=1)
                v_ref[l, k * B : (k + 1) * B, :] = v.astype(BF16)
            if meanwhile is not None:
                meanwhile(2 * k)
                meanwhile(2 * k + 1)
        for chunk in range(CHUNKS):
            size = U // CHUNKS
            rows = slice(chunk * size, (chunk + 1) * size)
            for l in range(4):
                parts = [
                    v_ref[l, k * B + u * U + chunk * size : k * B + u * U + (chunk + 1) * size, :]
                    for k in range(4)
                    for u in range(2)
                ]
                y = dot(jnp.concatenate(parts, axis=0), right[l])
                for k in range(4):
                    for c in range(2):
                        at = y[2 * k * size : (2 * k + 2) * size, lanes(c)]
                        both = jnp.concatenate([at[:size], at[size:]], axis=1)
                        y_ref[c, k, rows, wide(l)] = both.astype(BF16)
            if chunk:
                for s in range(STRIPS // CHUNKS):
                    strip((chunk - 1) * (STRIPS // CHUNKS) + s)
        for s in range(STRIPS // CHUNKS):
            strip((CHUNKS - 1) * (STRIPS // CHUNKS) + s)

    def masked(plane, field, k, l, s):
        g = mul(field, load(mask_ref.at[plane], k, l, s))
        store(g_ref.at[plane], k, l, s, g)
        return g

    def first_strip(s):
        decode(0, s)

        def at(k, l):
            field = (source_x[k, rows_of(s), :] * source_y[l, 0:1]).astype(BF16)
            mask = load(mask_ref.at[0], k, l, s)
            g = (field * mask[0], field * mask[1])
            store(g_ref.at[0], k, l, s, g)
            return g

        spread_out([[at(k, l) for l in range(4)] for k in range(4)], s)

    def forward_strip(plane, s):
        field = gathered_up(s)
        spread_out([[masked(plane, field[k][l], k, l, s) for l in range(4)] for k in range(4)], s)

    def last_strip(s):
        field = gathered_up(s)
        for k in range(4):
            a = (far_x[0, k, rows_of(s), :], far_x[1, k, rows_of(s), :])
            for l in range(4):
                part = mul(masked(PLANES - 1, field[k][l], k, l, s), a)
                sums[l] = add(sums[l], (part[0].astype(F32), part[1].astype(F32)))

    def returned(plane, back, k, l, s):
        g = load(g_ref.at[plane], k, l, s)
        half, group, rows = piece_of(k, s)
        grad[half, (k % 2) * GROUPS + group + l // 2, plane, l % 2, rows] = back[0] * g[1] + back[1] * g[0]
        return mul(back, load(mask_ref.at[plane], k, l, s)) if plane else None

    for s in range(STRIPS):
        first_strip(s)
    for plane in range(1, PLANES - 1):
        operate(functools.partial(forward_strip, plane), functools.partial(decode, plane))
    nothing = jnp.zeros((STRIP, W), F32)
    sums = [(nothing, nothing) for _ in range(4)]
    operate(last_strip, functools.partial(decode, PLANES - 1))
    far = [(far_y[0, l], far_y[1, l]) for l in range(4)]
    total = [mul(s, y) for s, y in zip(sums, far)]
    coupling_re = jnp.sum(sum(t[0] for t in total))
    coupling_im = jnp.sum(sum(t[1] for t in total))
    back_y = [
        (
            (coupling_re * y[0] + coupling_im * y[1]).astype(BF16),
            (coupling_re * y[1] - coupling_im * y[0]).astype(BF16),
        )
        for y in far
    ]

    def turn_strip(s):
        def at(k, l):
            a = (far_x[0, k, rows_of(s), :], far_x[1, k, rows_of(s), :])
            return returned(PLANES - 1, mul(a, back_y[l]), k, l, s)

        spread_out([[at(k, l) for l in range(4)] for k in range(4)], s)

    def backward_strip(plane, s):
        back = gathered_up(s)
        reply = [[returned(plane, back[k][l], k, l, s) for l in range(4)] for k in range(4)]
        if plane:
            spread_out(reply, s)

    for s in range(STRIPS):
        turn_strip(s)
    for plane in reversed(range(PLANES - 1)):
        operate(functools.partial(backward_strip, plane))
    departures = [
        pltpu.make_async_copy(grad.at[1 - core], send, sems.at[0]),
        pltpu.make_async_copy(grad.at[core], keep, sems.at[1]),
    ]
    for copy in departures:
        copy.start()
    for copy in departures:
        copy.wait()


def main_call(plane_id, core_id, side_id, tan_own, tan_in, tables):
    half = (2 * GROUPS, PLANES, 2, *PIECE)
    return pl.pallas_call(
        main_kernel,
        name="modes",
        in_specs=[SMEM] * 3 + [VMEM] * 19,
        out_specs=[ANY, ANY],
        out_shape=[jax.ShapeDtypeStruct(half, BF16)] * 2,
        scratch_shapes=[
            pltpu.VMEM((2, 4, U, WIDE), BF16),
            pltpu.VMEM((4, N, 2 * B), BF16),
            pltpu.VMEM((2, 4, U, WIDE), BF16),
            pltpu.VMEM((PLANES, 2, 4, U, WIDE), BF16),
            pltpu.VMEM((PLANES, 2, 4, U, WIDE), BF16),
            pltpu.VMEM((PLANES, 2, 2, GROUPS, 2, *PIECE), BF16),
            pltpu.VMEM((2, *half), BF16),
            pltpu.SemaphoreType.DMA((2,)),
        ],
        compiler_params=vmem_limit(26),
    )(plane_id, core_id, side_id, tan_own, *tan_in, *tables)


def tangents_of_strip(phase, first, r, out):
    for u in range(2):
        rows = slice(first + u * U + r * PIECE[0], first + u * U + (r + 1) * PIECE[0])
        for l in range(4):
            out[2 * r + l // 2, l % 2, :, lanes(u)] = half_angle_tangent(phase[rows, lanes(l)]).astype(BF16)


def tangent_kernel(row_id, phase, out, rows, tangents, sems_in, sems_out):
    strips = U // PIECE[0]
    arrivals, departures = [], []
    for r in range(strips):
        for u in range(2):
            at = pl.ds(row_id[0] * B + u * U + r * PIECE[0], PIECE[0])
            here = rows.at[u * U + r * PIECE[0] : u * U + (r + 1) * PIECE[0]]
            arrivals.append(pltpu.make_async_copy(phase.at[0, at], here, sems_in.at[2 * r + u]))
        pair = slice(2 * r, 2 * r + 2)
        departures.append(pltpu.make_async_copy(tangents.at[pair], out.at[pair], sems_out.at[r]))
    for copy in arrivals:
        copy.start()
    for r in range(strips):
        arrivals[2 * r].wait()
        arrivals[2 * r + 1].wait()
        tangents_of_strip(rows, 0, r, tangents)
        departures[r].start()
    for copy in departures:
        copy.wait()


def tangent_call(row_id, phase_masks):
    return pl.pallas_call(
        tangent_kernel,
        name="tangent",
        in_specs=[SMEM, HBM],
        out_specs=HBM,
        out_shape=jax.ShapeDtypeStruct((GROUPS, 2, *PIECE), BF16),
        scratch_shapes=[
            pltpu.VMEM((B, N), F32),
            pltpu.VMEM((GROUPS, 2, *PIECE), BF16),
            pltpu.SemaphoreType.DMA((2 * U // PIECE[0],)),
            pltpu.SemaphoreType.DMA((U // PIECE[0],)),
        ],
        compiler_params=vmem_limit(59),
    )(row_id, phase_masks)


def own_tangent_kernel(phase, out):
    def row(k, carry):
        for r in range(U // PIECE[0]):
            tangents_of_strip(phase.at[0, pl.ds(pl.multiple_of(k * B, B), B)], 0, r, out.at[k // 2, k % 2])
        return carry

    lax.fori_loop(0, 4, row, 0)


def own_tangent_call(phase_masks):
    return pl.pallas_call(
        own_tangent_kernel,
        name="own_tangent",
        in_specs=[VMEM],
        out_specs=VMEM,
        out_shape=jax.ShapeDtypeStruct((2, 2, GROUPS, 2, *PIECE), BF16),
        compiler_params=vmem_limit(6),
    )(phase_masks)


def rows_of_group(half, group, u):
    k, r = 2 * half + group // GROUPS, (group % GROUPS) // 2
    return pl.ds(k * B + u * U + r * PIECE[0], PIECE[0])


def cols_of_group(group, n):
    return lanes(2 * (group % 2) + n)


def finish_kernel(core_id, phase, own, other, out, result, sems):
    squares = jnp.zeros(PIECE, F32)
    for group in range(2 * GROUPS):
        for n in range(2):
            for part in (own, other):
                x = part[group, n].astype(F32)
                squares += x * x
    mean = 4.0 * jnp.sum(squares, keepdims=True) / (N * N)
    scale = -2.0 * lax.rsqrt(mean + EPSILON)
    core = core_id[0]
    departures = []
    for part, half in ((own, core), (other, 1 - core)):
        for side in range(2):
            for group in range(side * GROUPS, (side + 1) * GROUPS):
                for n in range(2):
                    for u in range(2):
                        rows, cols = rows_of_group(half, group, u), cols_of_group(group, n)
                        step = part[group, n, :, lanes(u)].astype(F32) * scale
                        result[rows, cols] = phase[0, rows, cols] + step
            done = pl.ds(pl.multiple_of((2 * half + side) * B, B), B)
            copy = pltpu.make_async_copy(result.at[done], out.at[0, done], sems.at[len(departures)])
            copy.start()
            departures.append(copy)
    for copy in departures:
        copy.wait()


def finish_call(core_id, phase_masks, own, other):
    return pl.pallas_call(
        finish_kernel,
        name="finish",
        in_specs=[SMEM, VMEM, VMEM, VMEM],
        out_specs=HBM,
        out_shape=jax.ShapeDtypeStruct((1, N, N), F32),
        scratch_shapes=[pltpu.VMEM((N, N), F32), pltpu.SemaphoreType.DMA((4,))],
        compiler_params=vmem_limit(8),
    )(core_id, phase_masks, own, other)


def swapped(x):
    return lax.ppermute(x, CORE, [(0, 1), (1, 0)])


def shifted(x, step):
    return lax.ppermute(x, "mode_0", [(i, (i + step) % 4) for i in range(4)])


def from_plane(x, step):
    across = 1 if step == 2 else 0
    here = [(p, z) for p in range(PLANES) for z in range(2)]
    there = [((p + step) % PLANES * 2 + (z ^ across), 2 * p + z) for p, z in here]
    return lax.ppermute(x, Z, there)


def exchanged(x, axes):
    return lax.all_to_all(x, axes, split_axis=0, concat_axis=0, tiled=True)


def from_everyone(x, axes):
    count = lax.axis_size(axes)
    return exchanged(jnp.broadcast_to(x[None], (count, *x.shape)), axes)


def shards(phase_masks, hg_orders, spot_index):
    core_id = lax.axis_index(CORE).astype(jnp.int32)[None]
    plane_id = lax.axis_index("plane").astype(jnp.int32)[None]
    side_id = (lax.axis_index("mode_0").astype(jnp.int32) & 1)[None]
    tangent = tangent_call(2 * core_id + side_id, phase_masks)
    beside_own = [from_plane(tangent, step) for step in (1, -1)]
    opposite = from_plane(tangent, 2)
    tan_own = own_tangent_call(phase_masks)
    tables = setup_call(plane_id, hg_orders.T, spot_index, *block_operators())
    beside_own, tan_own, tables = lax.optimization_barrier((beside_own, tan_own, tables))
    beside_own = jnp.stack(beside_own)
    cut = GROUPS // 2
    half_own = [beside_own, shifted(beside_own[:, :cut], 1), shifted(beside_own[:, cut:], -1)]
    half_own += [opposite, shifted(opposite[:cut], 1), shifted(opposite[cut:], -1)]
    tan_in = half_own + [swapped(x) for x in half_own]
    keep, send = main_call(plane_id, core_id, side_id, tan_own, tan_in, tables)
    pair = keep + swapped(send)
    column = jnp.sum(exchanged(pair, XY).astype(F32), axis=0).astype(BF16)
    pieces = jnp.repeat(column, 2, axis=0)
    total = jnp.sum(exchanged(pieces, Z).astype(F32), axis=0).astype(BF16)
    own = from_everyone(total, XY)
    other = swapped(own)
    return finish_call(core_id, phase_masks, own, other)


def solution(mesh):
    finer = Mesh(
        mesh.devices.reshape(mesh.shape["plane"], 4, 4, 2, 2),
        ("plane", "mode_0", "mode_1", "mode_2", "mode_3"),
    )
    placed = (P("plane", None, None), P(MODE, None), P(MODE))
    return jax.shard_map(
        shards, mesh=finer, in_specs=placed, out_specs=P("plane", None, None), check_vma=False
    )
```
